32 devices in a mesh: rep: 4 (over y, core), own: 4 (over z), cp: 2 (over x).
Axes of the slice: x: 2, y: 2, z: 4, core: 2. Of those that a mesh axis runs over, the one named last changes fastest.
Arguments:
- tokens: bfloat16 [16, 1024, 576], P(('rep', 'own'), 'cp')
- cotangent: bfloat16 [16, 1024, 576], P(('rep', 'own'), 'cp'), may hold values from -6 to 6
- segment_ids: int32 [16, 1024], P(('rep', 'own'), 'cp'), may hold values from 0 to 3, as said below
- positions: int32 [16, 1024], P(('rep', 'own'), 'cp'), may hold values from 0 to 1020, as said below
- assignment: int32 [7], replicated, may hold values from 0 to 3, as said below
- weight_state: float32 [4, 1769472], P('own'), as said below
- momentum_state: float32 [4, 1769472], P('own'), may hold values from -40 to 40
- gains: float32 [2, 576], replicated, may hold values from 0.5 to 1.5
- gain_momentum: float32 [2, 576], replicated, may hold values from -384 to 384
Outputs:
- output: bfloat16 [16, 1024, 576], P(('rep', 'own'), 'cp')
- input_grad: float32 [16, 1024, 576], P(('rep', 'own'), 'cp')
- grad_state: float32 [4, 1769472], P('own')
- weight_new: float32 [4, 1769472], P('own')
- momentum_new: float32 [4, 1769472], P('own')
- gain_grad: float32 [2, 576], replicated
- gains_new: float32 [2, 576], replicated
- gain_moment: float32 [2, 576], replicated
The draws below stay inside these ranges and needn't reach their ends.
Inputs may be any that keep to these rules, and one draw needn't show every extreme that they name: `assignment`: each entry is an index along own; the three feed-forward matrices have three different owners, and one of these owns the four attention matrices as well. `segment_ids`: each sequence holds 4 documents, each a run of one or more consecutive tokens; numbers count up from 0 along a sequence. `positions`: 0 at a document's first token, rising by one along it. `weight_state`: entries of a row past its owner's matrices belong to no matrix.
All inputs are finite; a program needn't handle non-finite values.
Results may differ from the reference program's by a relative error of at most 0.014.
Values may be sent and summed in bfloat16 or wider, within the bound.
No kernel may reach another device: no remote copies, remote signals or barrier semaphores. Data moves between devices by JAX's collectives and lax.ppermute only.
A program may use at most 256 MiB of HBM per device.

```python
import math
import jax
import jax.numpy as jnp
from jax import lax

D = 576
HEADS = 9
KV_HEADS = 3
HEAD = 64
FF = 1536
QBLOCK = 512
DOCS = 4
LEN = 1024
SEQS = 16
OWNERS = 4
CAP = 1769472
N_OWN = 4


def owner_plan(key):
    base = jax.random.fold_in(key, 71)
    first_key, second_key, third_key = jax.random.split(base, 3)
    middle_owner = jax.random.randint(first_key, (), 1, N_OWN - 1)
    chosen = jnp.stack([jnp.zeros((), jnp.int32), middle_owner.astype(jnp.int32), jnp.zeros((), jnp.int32) + (N_OWN - 1)])
    shuffled = jax.random.permutation(second_key, 3)
    feed_owners = chosen[shuffled].astype(jnp.int32)
    choose = jax.random.randint(third_key, (), 0, 3)
    leader = feed_owners[choose]
    return jnp.concatenate([jnp.zeros((4,), jnp.int32) + leader, feed_owners]).astype(jnp.int32)


def draw_assignment(key, part):
    return owner_plan(key)


def region_scales(owners, focus):
    kv_width = KV_HEADS * HEAD
    sizes_list = [D * HEADS * HEAD, D * kv_width, D * kv_width, HEADS * HEAD * D, D * FF, D * FF, FF * D]
    entries = jnp.array(sizes_list, jnp.int32)
    order = jnp.arange(7)
    earlier = (owners[:, None] == owners[None, :]) & (order[None, :] < order[:, None])
    starts = jnp.sum(jnp.where(earlier, entries[None, :], 0), axis=1).astype(jnp.int32)
    column = jnp.arange(CAP, dtype=jnp.int32)[None, :]
    line = jnp.arange(N_OWN, dtype=jnp.int32)[:, None]
    scaling = jnp.zeros((N_OWN, CAP), jnp.float32) + D ** (-0.5)
    for matrix in range(7):
        inside = (line == owners[matrix]) & (column >= starts[matrix]) & (column < starts[matrix] + entries[matrix])
        scaling = jnp.where(inside, focus[matrix], scaling)
    return scaling


def draw_weight_state(key, part):
    owners = owner_plan(key)
    noise_key = jax.random.fold_in(key, 5)
    noise = jax.random.normal(noise_key, (N_OWN, CAP), jnp.float32)
    base = D ** (-0.5)
    focus = [base, base, base, 5.0 * base, base, base, FF ** (-0.5)]
    return noise * region_scales(owners, focus)


def draw_tokens(key, part):
    base = jax.random.fold_in(key, 3)
    noise_key, scale_key = jax.random.split(base)
    noise = jax.random.normal(noise_key, (SEQS, LEN, D), jnp.float32)
    spread = jnp.exp(jax.random.uniform(scale_key, (SEQS, LEN, 1), jnp.float32, math.log(0.5), math.log(5.0)))
    return (noise * spread).astype(jnp.bfloat16)


def document_cuts(key):
    base = jax.random.fold_in(key, 29)
    row_keys = jax.random.split(base, SEQS)

    def one_row(row_key):
        return jnp.sort(jax.random.permutation(row_key, LEN - 1)[:DOCS - 1] + 1).astype(jnp.int32)
    random_cuts = jax.vmap(one_row)(row_keys)
    longest = (LEN - DOCS + 1 + jnp.arange(DOCS - 1, dtype=jnp.int32)).astype(jnp.int32)
    first_row = (jnp.arange(SEQS, dtype=jnp.int32) == 0)[:, None]
    return jnp.where(first_row, longest[None, :], random_cuts).astype(jnp.int32)


def draw_segment_ids(key, part):
    cuts = document_cuts(key)
    index = jnp.arange(LEN, dtype=jnp.int32)
    return jnp.sum((index[None, :, None] >= cuts[:, None, :]).astype(jnp.int32), axis=-1).astype(jnp.int32)


def draw_positions(key, part):
    cuts = document_cuts(key)
    index = jnp.arange(LEN, dtype=jnp.int32)
    begins = jnp.max(jnp.where(index[None, :, None] >= cuts[:, None, :], cuts[:, None, :], 0), axis=-1)
    return (index[None, :] - begins).astype(jnp.int32)


def block_levels(key, dims, cuts, smallest, top_value):
    level, own = 1.0, jax.random.fold_in(key, 6)
    for axis_at, parts in cuts:
        draws = jnp.exp(jax.random.uniform(jax.random.fold_in(own, axis_at), (parts,), jnp.float32, smallest / len(cuts), top_value / len(cuts)))
        level = level * jnp.repeat(draws, dims[axis_at] // parts).reshape([-1 if axis == axis_at else 1 for axis in range(len(dims))])
    return level


def normal_values(stream_key, shape, scale, limit, cuts=(), kind=jnp.bfloat16):
    factor_of = block_levels(stream_key, shape, cuts, -0.22, 0.18) if cuts else 1.0
    values = jax.random.normal(stream_key, shape, jnp.float32) * scale * factor_of
    return jnp.minimum(jnp.maximum(values, -limit), limit).astype(kind)


def setup_inputs(seed: int = 0) -> dict:
    splits = jax.random.split(jax.random.key(seed), 10)
    tokens = draw_tokens(jax.random.fold_in(splits[9], 71), 0)
    cotangent = normal_values(splits[1], (SEQS, LEN, D), 1.0, 6.0, ((0, 16), (1, 2)))
    segment_ids = draw_segment_ids(jax.random.fold_in(splits[9], 71), 0)
    positions = draw_positions(jax.random.fold_in(splits[9], 71), 0)
    assignment = draw_assignment(jax.random.fold_in(splits[9], 71), 0)
    weight_state = draw_weight_state(jax.random.fold_in(splits[9], 71), 0)
    momentum_state = normal_values(splits[6], (OWNERS, CAP), (0.05 * (SEQS * LEN) ** 0.5), 40.0, ((0, 4),), jnp.float32)
    gains = jnp.clip(1.0 + 0.1 * jax.random.normal(splits[7], (2, D), jnp.float32), 0.5, 1.5)
    gain_momentum = normal_values(splits[8], (2, D), (0.5 * (SEQS * LEN) ** 0.5), 384.0, (), jnp.float32)
    return dict(tokens=tokens, cotangent=cotangent, segment_ids=segment_ids, positions=positions, assignment=assignment, weight_state=weight_state, momentum_state=momentum_state, gains=gains, gain_momentum=gain_momentum)


EPSILON = 1e-05
MOMENTUM = 0.95
LEARN_RATE = 0.05
GAIN_RATE = 0.1
ROPE_BASE = 10000.0
QUINTIC_A = 3.4445
QUINTIC_B = -4.775
QUINTIC_C = 2.0315
HIGHEST = lax.Precision.HIGHEST

@jax.custom_vjp
def low(v):
    return lax.optimization_barrier(v.astype(jnp.bfloat16)).astype(jnp.float32)

@jax.custom_vjp
def low_back(v):
    return v

def low_keep(v):
    return (low(v), None)

def low_pass(kept, grad):
    return (grad,)

def back_keep(v):
    return (v, None)

def back_low(kept, grad):
    return (low(grad),)
low.defvjp(low_keep, low_pass)
low_back.defvjp(back_keep, back_low)

def matrix_shapes():
    kv_width = KV_HEADS * HEAD
    return [(D, HEADS * HEAD), (D, kv_width), (D, kv_width), (HEADS * HEAD, D), (D, FF), (D, FF), (FF, D)]

def region_starts(assignment):
    entries = jnp.array([height * breadth for height, breadth in matrix_shapes()], jnp.int32)
    order = jnp.arange(7)
    earlier = (assignment[:, None] == assignment[None, :]) & (order[None, :] < order[:, None])
    return lax.optimization_barrier(jnp.sum(jnp.where(earlier, entries[None, :], 0), axis=1)).astype(jnp.int32)

def take_region(state, owner, start_at, shape):
    line = lax.dynamic_index_in_dim(state, owner, 0, keepdims=False)
    return lax.dynamic_slice_in_dim(line, start_at, shape[0] * shape[1]).reshape(shape)

def put_region(state, owner, start_at, matrix_value):
    return lax.dynamic_update_slice(state, matrix_value.reshape(1, -1), (owner.astype(jnp.int32), start_at.astype(jnp.int32)))

def rotate(matrix_value, places, direction):
    half_head = HEAD // 2
    frequency = ROPE_BASE ** (-(jnp.arange(half_head, dtype=jnp.float32) * 2.0 / HEAD))
    angles = places.astype(jnp.float32)[..., None] * frequency
    cosine = jnp.cos(angles)[..., None, :]
    sines = direction * jnp.sin(angles)[..., None, :]
    shaped = matrix_value.reshape(matrix_value.shape[:-1] + (-1, HEAD))
    first_half = shaped[..., :half_head]
    second_half = shaped[..., half_head:]
    turned = jnp.concatenate([first_half * cosine - second_half * sines, second_half * cosine + first_half * sines], axis=-1)
    return turned.reshape(matrix_value.shape)

def rms_normalize(values, gain):
    factor = lax.rsqrt(lax.optimization_barrier(jnp.mean(values * values, axis=-1, keepdims=True)) + EPSILON)
    return values * factor * gain

def project(inputs, weight):
    return jnp.einsum('bld,de->ble', inputs, weight, precision=HIGHEST)

def attention(queries, key_rows, value_rows, segments):
    batch, length = queries.shape[:2]
    share = HEADS // KV_HEADS
    block_count = length // QBLOCK
    query_heads = queries.reshape(batch, block_count, QBLOCK, KV_HEADS, share, HEAD)
    query_blocks = jnp.moveaxis(query_heads, 1, 0)
    segment_blocks = jnp.moveaxis(segments.reshape(batch, block_count, QBLOCK), 1, 0)
    block_starts = (jnp.arange(block_count) * QBLOCK).astype(jnp.int32)
    key_heads = key_rows.reshape(batch, length, KV_HEADS, HEAD)
    value_heads = value_rows.reshape(batch, length, KV_HEADS, HEAD)
    key_order = jnp.arange(length).astype(jnp.int32)

    @jax.checkpoint
    def one_block(item):
        block_queries, block_segments, start_at = item
        scores = jnp.einsum('bqgrd,bkgd->bgrqk', block_queries, key_heads, precision=HIGHEST) * HEAD ** (-0.5)
        scores = low_back(scores)
        query_order = start_at + jnp.arange(QBLOCK).astype(jnp.int32)
        allowed = (key_order[None, :] <= query_order[:, None])[None] & (block_segments[:, :, None] == segments[:, None, :])
        scores = jnp.where(allowed[:, None, None], scores, -jnp.inf)
        weights = low(jax.nn.softmax(scores, axis=-1))
        return jnp.einsum('bgrqk,bkgd->bqgrd', weights, value_heads, precision=HIGHEST)
    mixed_blocks = lax.map(one_block, (query_blocks, segment_blocks, block_starts))
    mixed_heads = jnp.moveaxis(mixed_blocks, 0, 1)
    return mixed_heads.reshape(batch, length, HEADS * HEAD)

def layer(inputs, weights, gains, segments, places):
    weight_q, weight_k, weight_v, weight_o, weight_gate, weight_up, weight_down = weights
    normed_one = low(rms_normalize(inputs, gains[0]))
    queries = low(rotate(low_back(project(normed_one, weight_q)), places, 1.0))
    key_rows = low(rotate(low_back(project(normed_one, weight_k)), places, 1.0))
    value_rows = low_back(low(project(normed_one, weight_v)))
    mixed_out = low_back(low(attention(queries, key_rows, value_rows, segments)))
    middle = inputs + low_back(project(mixed_out, weight_o))
    normed_two = low(rms_normalize(middle, gains[1]))
    gate_proj = low_back(project(normed_two, weight_gate))
    up_proj = low_back(project(normed_two, weight_up))
    hidden = low(jax.nn.silu(gate_proj) * up_proj)
    return middle + low_back(project(hidden, weight_down))

def orthogonalize(matrix_value):
    tall = matrix_value.shape[0] > matrix_value.shape[1]
    work = matrix_value.T if tall else matrix_value
    work = (work / (jnp.sqrt(jnp.sum(work * work)) + 1e-07)).astype(jnp.bfloat16)
    for repeat in range(5):
        square = jnp.dot(work, work.T, preferred_element_type=jnp.float32).astype(jnp.bfloat16)
        mixer = (QUINTIC_B * square.astype(jnp.float32) + QUINTIC_C * jnp.dot(square, square, preferred_element_type=jnp.float32)).astype(jnp.bfloat16)
        work = (QUINTIC_A * work.astype(jnp.float32) + jnp.dot(mixer, work, preferred_element_type=jnp.float32)).astype(jnp.bfloat16)
    result = work.astype(jnp.float32)
    return result.T if tall else result

def reference(tokens, cotangent, segment_ids, positions, assignment, weight_state, momentum_state, gains, gain_momentum):
    shapes = matrix_shapes()
    starts = region_starts(assignment)
    masters = [take_region(weight_state, assignment[matrix], starts[matrix], shapes[matrix]) for matrix in range(7)]
    rounded = [low(master) for master in masters]

    def grouped(array):
        return array.reshape((SEQS, 1) + array.shape[1:])

    def one_group(totals, batch):
        block_tokens, block_cotangent, block_segments, block_places = batch

        def forward(inputs, *params):
            return layer(inputs, params[:7], params[7], block_segments, block_places)
        result, pull = jax.vjp(forward, block_tokens.astype(jnp.float32), *rounded, gains)
        pulled = pull(block_cotangent.astype(jnp.float32))
        totals = tuple((previous + fresh for previous, fresh in zip(totals, pulled[1:])))
        return (totals, (result.astype(jnp.bfloat16), pulled[0]))
    initial = tuple((jnp.zeros_like(weight) for weight in rounded)) + (jnp.zeros_like(gains),)
    totals, outs = lax.scan(one_group, initial, (grouped(tokens), grouped(cotangent), grouped(segment_ids), grouped(positions)))
    output = outs[0].reshape(tokens.shape)
    input_grad = outs[1].reshape(tokens.shape)
    grad_state = jnp.zeros_like(weight_state)
    weight_new = weight_state
    momentum_new = momentum_state
    for matrix in range(7):
        gradient = totals[matrix]
        moment = MOMENTUM * take_region(momentum_state, assignment[matrix], starts[matrix], shapes[matrix]) + gradient
        nesterov = gradient + MOMENTUM * moment
        orthogonal = orthogonalize(nesterov)
        step_scale = LEARN_RATE * 0.2 * math.sqrt(max(shapes[matrix]))
        updated = masters[matrix] - step_scale * orthogonal
        grad_state = put_region(grad_state, assignment[matrix], starts[matrix], gradient)
        weight_new = put_region(weight_new, assignment[matrix], starts[matrix], updated)
        momentum_new = put_region(momentum_new, assignment[matrix], starts[matrix], moment)
    gain_grad = totals[7]
    gain_moment = MOMENTUM * gain_momentum + gain_grad
    push_gain = gain_grad + MOMENTUM * gain_moment
    gains_new = gains - GAIN_RATE * push_gain * lax.rsqrt(lax.optimization_barrier(jnp.mean(push_gain * push_gain, axis=-1, keepdims=True)) + 1e-06)
    return (output, input_grad, grad_state, weight_new, momentum_new, gain_grad, gains_new, gain_moment)
```

```python
import functools
import math

import jax
import jax.numpy as jnp
from jax import lax
from jax.experimental import pallas as pl
from jax.experimental.pallas import tpu as pltpu
from jax.sharding import PartitionSpec as P

D = 576
HEADS = 9
KV_HEADS = 3
HEAD = 64
FF = 1536
QBLOCK = 512


EPSILON = 1e-05
MOMENTUM = 0.95
LEARN_RATE = 0.05
GAIN_RATE = 0.1
ROPE_BASE = 10000.0
QUINTIC_A = 3.4445
QUINTIC_B = -4.775
QUINTIC_C = 2.0315


def from_behind(block, axis, distance):
    devices = range(lax.axis_size(axis))
    route = [(i - distance, i) for i in devices if i - distance in devices]
    return lax.ppermute(block, axis, route)


def product(left, right):
    return jnp.dot(left, right, preferred_element_type=jnp.float32)


def over_rows(left, right):
    return lax.dot_general(
        left, right, (((0,), (0,)), ((), ())), preferred_element_type=jnp.float32
    )


def against(left, right):
    return lax.dot_general(
        left, right, (((1,), (1,)), ((), ())), preferred_element_type=jnp.float32
    )


def rotate(matrix_value, places, direction):
    half_head = HEAD // 2
    frequency = ROPE_BASE ** (-(jnp.arange(half_head, dtype=jnp.float32) * 2.0 / HEAD))
    angles = places.astype(jnp.float32)[..., None] * frequency
    cosine = jnp.cos(angles)[..., None, :]
    sines = direction * jnp.sin(angles)[..., None, :]
    shaped = matrix_value.reshape(matrix_value.shape[:-1] + (-1, HEAD))
    first_half = shaped[..., :half_head]
    second_half = shaped[..., half_head:]
    turned = jnp.concatenate(
        [first_half * cosine - second_half * sines, second_half * cosine + first_half * sines],
        axis=-1,
    )
    return turned.reshape(matrix_value.shape)


def rms_normalize(values, gain):
    factor = lax.rsqrt(jnp.mean(values * values, axis=-1, keepdims=True) + EPSILON)
    return values * factor * gain


def norm_backward(values, gain, upstream):
    factor = lax.rsqrt(jnp.mean(values * values, axis=-1, keepdims=True) + EPSILON)
    normed = values * factor
    scaled = upstream * gain
    gain_part = jnp.sum(upstream * normed, axis=0)
    inputs_part = factor * (scaled - normed * jnp.mean(scaled * normed, axis=-1, keepdims=True))
    return (inputs_part, gain_part)


F32 = jnp.float32
BF16 = jnp.bfloat16
LANES = 128
HALF_ROWS = D // 2
PIECE_ROWS = D * FF // LANES
CHUNKS = FF // LANES
STEP_SCALE_FF = LEARN_RATE * 0.2 * math.sqrt(FF)
STEP_SCALE_ATTN = LEARN_RATE * 0.2 * math.sqrt(D)
VMEM_LIMIT = 60 << 20
VMEM_SPEC = pl.BlockSpec(memory_space=pltpu.VMEM)
SMEM_SPEC = pl.BlockSpec(memory_space=pltpu.SMEM)
ANY_SPEC = pl.BlockSpec(memory_space=pl.ANY)
Q_AT, K_AT, V_AT, O_AT = 0, 2592, 3456, 4320
Q_ROWS, K_ROWS = 2592, 864


def turn(value):
    return pltpu.roll(value, 64, 1)


def join(low, high):
    lane = lax.broadcasted_iota(jnp.int32, low.shape, 1)
    return jnp.where(lane < 64, low, high)


def rows_to_columns(take):
    even = [lambda k=k: take(k) for k in range(5)]
    odd = [lambda k=k: join(turn(take(4 + k)), turn(take(5 + k))) for k in range(4)]
    odd.append(lambda: turn(take(8)))
    return even, odd


def columns_to_rows(even, odd):
    lines = [lambda k=k: even(k) for k in range(4)]
    lines.append(lambda: join(even(4), turn(odd(0))))
    for k in range(1, 5):
        lines.append(lambda k=k: join(turn(odd(k - 1)), turn(odd(k))))
    return lines


def attention_chunks(q, k, v, o):
    even = [lambda i=i: q(i) for i in range(4)]
    even.append(lambda: join(q(4), turn(k(0))))
    even.append(lambda: join(turn(k(0)), turn(k(1))))
    even.append(lambda: v(0))
    even.append(lambda: join(v(1), turn(o(4))))
    even += [lambda i=i: o(i) for i in range(4)]
    odd = [lambda i=i: join(turn(q(4 + i)), turn(q(5 + i))) for i in range(4)]
    odd.append(lambda: join(turn(q(8)), k(1)))
    odd.append(lambda: k(2))
    odd.append(lambda: join(turn(v(1)), turn(v(2))))
    odd.append(lambda: join(turn(v(2)), o(8)))
    odd += [lambda i=i: join(turn(o(4 + i)), turn(o(5 + i))) for i in range(4)]
    return even, odd


def attention_lines(even, odd):
    q = columns_to_rows(even, odd)
    k = [
        lambda: join(turn(even(4)), turn(even(5))),
        lambda: join(turn(even(5)), odd(4)),
        lambda: odd(5),
    ]
    v = [
        lambda: even(6),
        lambda: join(even(7), turn(odd(6))),
        lambda: join(turn(odd(6)), turn(odd(7))),
    ]
    o = [lambda i=i: even(8 + i) for i in range(4)]
    o.append(lambda: join(turn(even(7)), turn(odd(8))))
    for i in range(1, 4):
        o.append(lambda i=i: join(turn(odd(7 + i)), turn(odd(8 + i))))
    o.append(lambda: join(turn(odd(11)), odd(7)))
    return q, k, v, o


def extract_first_kernel(scal, state, out, qb, kb, vb, ob, mat, sems):
    core, quarter = scal[0], scal[1]
    copies = []
    for n, (buf, at, rows) in enumerate(
        ((qb, Q_AT, Q_ROWS // 2), (kb, K_AT, K_ROWS // 2), (vb, V_AT, K_ROWS // 2), (ob, O_AT, Q_ROWS // 2))
    ):
        begin = pl.multiple_of(at + rows * core, 8)
        copies.append(pltpu.make_async_copy(state.at[pl.ds(begin, rows)], buf, sems.at[n]))
    for copy in copies:
        copy.start()
    for copy in copies:
        copy.wait()
    pairs = HALF_ROWS // 2
    q = lambda i: qb[pl.ds(i, pairs, stride=9), :]
    k = lambda i: kb[pl.ds(i, pairs, stride=3), :]
    v = lambda i: vb[pl.ds(i, pairs, stride=3), :]
    o = lambda i: ob[pl.ds(i, pairs, stride=9), :]
    even, odd = attention_chunks(q, k, v, o)
    for at in range(4):

        @pl.when(quarter == at)
        def _(at=at):
            for j in range(2):
                mat[pl.ds(0, pairs, stride=2), :] = even[2 * at + j]()
                mat[pl.ds(1, pairs, stride=2), :] = odd[2 * at + j]()
                out[:, j * LANES : (j + 1) * LANES] = mat[...].astype(BF16)


def extract_first(scal, state):
    return pl.pallas_call(
        extract_first_kernel,
        out_shape=jax.ShapeDtypeStruct((HALF_ROWS, 2 * LANES), BF16),
        in_specs=[SMEM_SPEC, ANY_SPEC],
        out_specs=VMEM_SPEC,
        scratch_shapes=[
            pltpu.VMEM((Q_ROWS // 2, LANES), F32),
            pltpu.VMEM((K_ROWS // 2, LANES), F32),
            pltpu.VMEM((K_ROWS // 2, LANES), F32),
            pltpu.VMEM((Q_ROWS // 2, LANES), F32),
            pltpu.VMEM((HALF_ROWS, LANES), F32),
            pltpu.SemaphoreType.DMA((4,)),
        ],
        compiler_params=pltpu.CompilerParams(vmem_limit_bytes=VMEM_LIMIT),
        name="extract_first",
    )(scal, state)


def extract_rest_kernel(scal, state, wo_out, ff_out, ob, fb, db, mat, cols, turned, sems):
    core, quarter, half, is_down = scal[0], scal[1], scal[2], scal[4]
    pairs = HALF_ROWS // 2
    copy_o = pltpu.make_async_copy(
        state.at[pl.ds(pl.multiple_of(O_AT + Q_ROWS // 2 * core, 8), Q_ROWS // 2)], ob, sems.at[0]
    )
    copy_o.start()

    @pl.when(is_down == 0)
    def _():
        begin = pl.multiple_of(half * PIECE_ROWS + core * (PIECE_ROWS // 2), 8)
        copy = pltpu.make_async_copy(state.at[pl.ds(begin, PIECE_ROWS // 2)], fb, sems.at[1])
        copy.start()
        copy.wait()
        for at in range(4):

            @pl.when(quarter == at)
            def _(at=at):
                for j in range(3):
                    ff_out[:, j * LANES : (j + 1) * LANES] = fb[
                        pl.ds(3 * at + j, HALF_ROWS, stride=CHUNKS), :
                    ].astype(BF16)

    @pl.when(is_down != 0)
    def _():
        begin = pl.multiple_of(half * PIECE_ROWS + quarter * (PIECE_ROWS // 4), 8)
        copy = pltpu.make_async_copy(state.at[pl.ds(begin, PIECE_ROWS // 4)], db, sems.at[1])
        copy.start()
        copy.wait()
        even, odd = rows_to_columns(lambda i: db[pl.ds(i, 192, stride=9), :])
        for k in range(5):
            cols[pl.ds(0, 192, stride=2), :] = even[k]()
            cols[pl.ds(1, 192, stride=2), :] = odd[k]()
            turned[pl.ds(k * LANES, LANES), :] = cols[...].T
        ff_out[...] = turned[pl.ds(pl.multiple_of(core * HALF_ROWS, 8), HALF_ROWS), :].astype(BF16)

    copy_o.wait()
    even, odd = rows_to_columns(lambda i: ob[pl.ds(i, pairs, stride=9), :])
    for at in range(4):

        @pl.when(quarter == at)
        def _(at=at):
            mat[pl.ds(0, pairs, stride=2), :] = even[at]()
            mat[pl.ds(1, pairs, stride=2), :] = odd[at]()
            wo_out[...] = mat[...].astype(BF16)


def extract_rest(scal, state):
    return pl.pallas_call(
        extract_rest_kernel,
        out_shape=(
            jax.ShapeDtypeStruct((HALF_ROWS, LANES), BF16),
            jax.ShapeDtypeStruct((HALF_ROWS, 3 * LANES), BF16),
        ),
        in_specs=[SMEM_SPEC, ANY_SPEC],
        out_specs=(VMEM_SPEC, VMEM_SPEC),
        scratch_shapes=[
            pltpu.VMEM((Q_ROWS // 2, LANES), F32),
            pltpu.VMEM((PIECE_ROWS // 2, LANES), F32),
            pltpu.VMEM((PIECE_ROWS // 4, LANES), F32),
            pltpu.VMEM((HALF_ROWS, LANES), F32),
            pltpu.VMEM((FF // 4, LANES), F32),
            pltpu.VMEM((5 * LANES, FF // 4), F32),
            pltpu.SemaphoreType.DMA((2,)),
        ],
        compiler_params=pltpu.CompilerParams(vmem_limit_bytes=VMEM_LIMIT),
        name="extract_rest",
    )(scal, state)


def assemble_kernel(scal, *refs):
    blocks, out = refs[:8], refs[8]
    core, quarter = scal[0], scal[1]
    width = blocks[0].shape[1]
    for other in range(2):
        for step in range(4):
            row = pl.multiple_of((core ^ other) * HALF_ROWS, 16)
            column = pl.multiple_of((quarter ^ step) * width, LANES)
            out[pl.ds(row, HALF_ROWS), pl.ds(column, width)] = blocks[4 * other + step][...]


def assemble(scal, blocks):
    width = blocks[0].shape[1]
    return pl.pallas_call(
        assemble_kernel,
        out_shape=jax.ShapeDtypeStruct((D, 4 * width), BF16),
        in_specs=[SMEM_SPEC] + [VMEM_SPEC] * 8,
        out_specs=VMEM_SPEC,
        compiler_params=pltpu.CompilerParams(vmem_limit_bytes=VMEM_LIMIT),
        name="assemble",
    )(scal, *blocks)


def quintic(x, square):
    return (
        QUINTIC_B * square.astype(F32)
        + QUINTIC_C * jnp.dot(square, square, preferred_element_type=F32)
    ).astype(BF16)


def wide_step(x_ref):
    x = x_ref[...]
    mixer = quintic(x, against(x, x).astype(BF16))
    x_ref[...] = (QUINTIC_A * x.astype(F32) + product(mixer, x)).astype(BF16)


def tall_step(x_ref):
    x = x_ref[...]
    mixer = quintic(x, over_rows(x, x).astype(BF16))
    x_ref[...] = (QUINTIC_A * x.astype(F32) + against(x, mixer)).astype(BF16)


BAND = 864


def momentum_pass(grad, moment, owned):
    def band(i, _):
        rows = pl.ds(pl.multiple_of(i * BAND, BAND), BAND)
        g = jnp.where(owned, grad[rows, :], 0.0)
        m = moment[rows, :]
        grad[rows, :] = g
        moment[rows, :] = jnp.where(owned, MOMENTUM * m + g, m)
        return 0

    lax.fori_loop(0, PIECE_ROWS // BAND, band, 0)


def gather_chunks(core, quarter, blocks, chunks, first, count):
    for other in range(2):
        for step in range(4):
            row = pl.multiple_of((core ^ other) * HALF_ROWS, 16)
            for k in range(count):
                at = first + count * (quarter ^ step) + k
                chunks[at, pl.ds(row, HALF_ROWS), :] = blocks[4 * other + step][
                    :, k * LANES : (k + 1) * LANES
                ].astype(F32)


def ff_lines_from_chunks(is_down, chunks, columns, lines):
    @pl.when(is_down == 0)
    def _():
        for k in range(CHUNKS):
            lines[pl.ds(k, D, stride=CHUNKS), :] = chunks[k]

    @pl.when(is_down != 0)
    def _():
        for k in range(CHUNKS):
            tall = chunks[k].T
            for j in range(5):
                width = min(LANES, D - j * LANES)
                columns[j, k * LANES : (k + 1) * LANES, :width] = tall[:, j * LANES : j * LANES + width]
        half = FF // 2
        getters = columns_to_rows(
            lambda j: columns[j, pl.ds(0, half, stride=2), :],
            lambda j: columns[j, pl.ds(1, half, stride=2), :],
        )
        for k in range(9):
            lines[pl.ds(k, half, stride=9), :] = getters[k]()


def ff_update_kernel(scal, *refs):
    blocks = refs[:8]
    state, grad_out, moment_out, ortho_out = refs[8:12]
    chunks, grad, moment, look, columns, x, sems = refs[12:]
    core, quarter, half, owned, is_down = scal[0], scal[1], scal[2], scal[3] != 0, scal[4]
    rows = pl.ds(pl.multiple_of(half * PIECE_ROWS, 8), PIECE_ROWS)
    fetch = pltpu.make_async_copy(state.at[rows], moment, sems.at[0])
    fetch.start()
    gather_chunks(core, quarter, blocks, chunks, 0, 3)
    ff_lines_from_chunks(is_down, chunks, columns, grad)
    fetch.wait()
    momentum_pass(grad, moment, owned)
    store_g = pltpu.make_async_copy(grad, grad_out.at[rows], sems.at[1])
    store_m = pltpu.make_async_copy(moment, moment_out.at[rows], sems.at[2])
    store_g.start()
    store_m.start()

    @pl.when(owned & (core == 0))
    def _():
        def ahead(lines):
            return grad[lines, :] + MOMENTUM * moment[lines, :]

        @pl.when(is_down == 0)
        def _():
            for k in range(CHUNKS):
                chunks[k] = ahead(pl.ds(k, D, stride=CHUNKS))

        @pl.when(is_down != 0)
        def _():
            even, odd = rows_to_columns(lambda i: ahead(pl.ds(i, FF // 2, stride=9)))
            for j in range(5):
                columns[j, pl.ds(0, FF // 2, stride=2), :] = even[j]()
                columns[j, pl.ds(1, FF // 2, stride=2), :] = odd[j]()
                width = min(LANES, D - j * LANES)
                for k in range(CHUNKS):
                    tall = columns[j, k * LANES : (k + 1) * LANES, :].T
                    chunks[k, j * LANES : j * LANES + width, :] = tall[:width, :]

        total = jnp.zeros((D, LANES), F32)
        for k in range(CHUNKS):
            total += chunks[k] * chunks[k]
        norm = jnp.sqrt(jnp.sum(total)) + 1e-07
        for k in range(CHUNKS):
            x[:, k * LANES : (k + 1) * LANES] = (chunks[k] / norm).astype(BF16)

        def step(_, carry):
            wide_step(x)
            return carry

        lax.fori_loop(0, 5, step, 0)
        for k in range(CHUNKS):
            chunks[k] = x[:, k * LANES : (k + 1) * LANES].astype(F32)
        ff_lines_from_chunks(is_down, chunks, columns, look)
        ortho_out[...] = look[...].astype(BF16)

    store_g.wait()
    store_m.wait()


def ff_update(scal, blocks, state):
    lines = state.shape[0]
    return pl.pallas_call(
        ff_update_kernel,
        out_shape=(
            jax.ShapeDtypeStruct((lines, LANES), F32),
            jax.ShapeDtypeStruct((lines, LANES), F32),
            jax.ShapeDtypeStruct((PIECE_ROWS, LANES), BF16),
        ),
        in_specs=[SMEM_SPEC] + [VMEM_SPEC] * 8 + [ANY_SPEC],
        out_specs=(ANY_SPEC, ANY_SPEC, VMEM_SPEC),
        scratch_shapes=[
            pltpu.VMEM((CHUNKS, D, LANES), F32),
            pltpu.VMEM((PIECE_ROWS, LANES), F32),
            pltpu.VMEM((PIECE_ROWS, LANES), F32),
            pltpu.VMEM((PIECE_ROWS, LANES), F32),
            pltpu.VMEM((5, FF, LANES), F32),
            pltpu.VMEM((D, FF), BF16),
            pltpu.SemaphoreType.DMA((3,)),
        ],
        compiler_params=pltpu.CompilerParams(vmem_limit_bytes=VMEM_LIMIT),
        name="ff_update",
    )(scal, *blocks, state)


def attention_lines_from_chunks(chunks, lines):
    pairs = D // 2
    parts = attention_lines(
        lambda j: chunks[j, pl.ds(0, pairs, stride=2), :],
        lambda j: chunks[j, pl.ds(1, pairs, stride=2), :],
    )
    for begin, getters in zip((Q_AT, K_AT, V_AT, O_AT), parts):
        for k, getter in enumerate(getters):
            lines[pl.ds(begin + k, pairs, stride=len(getters)), :] = getter()


def attention_update_kernel(scal, *refs):
    first, rest = refs[:8], refs[8:16]
    state, _, _, grad_out, moment_out, ortho_out = refs[16:22]
    chunks, grad, moment, look, xq, xk, xv, xo, sems = refs[22:]
    core, quarter, half, owned = scal[0], scal[1], 1 - scal[2], scal[5] != 0
    rows = pl.ds(pl.multiple_of(half * PIECE_ROWS, 8), PIECE_ROWS)
    fetch = pltpu.make_async_copy(state.at[rows], moment, sems.at[0])
    fetch.start()
    gather_chunks(core, quarter, first, chunks, 0, 2)
    gather_chunks(core, quarter, rest, chunks, 8, 1)
    attention_lines_from_chunks(chunks, grad)
    fetch.wait()
    momentum_pass(grad, moment, owned)
    store_g = pltpu.make_async_copy(grad, grad_out.at[rows], sems.at[1])
    store_m = pltpu.make_async_copy(moment, moment_out.at[rows], sems.at[2])
    store_g.start()
    store_m.start()

    @pl.when(owned & (core == 1))
    def _():
        pairs = D // 2

        def ahead(begin, stride):
            def take(i):
                lines = pl.ds(begin + i, pairs, stride=stride)
                return grad[lines, :] + MOMENTUM * moment[lines, :]

            return take

        even, odd = attention_chunks(ahead(Q_AT, 9), ahead(K_AT, 3), ahead(V_AT, 3), ahead(O_AT, 9))
        for k in range(CHUNKS):
            chunks[k, pl.ds(0, pairs, stride=2), :] = even[k]()
            chunks[k, pl.ds(1, pairs, stride=2), :] = odd[k]()

        def low_half(value):
            return join(value, jnp.zeros_like(value))

        def start(x, parts):
            total = jnp.zeros((D, LANES), F32)
            for part in parts:
                value = part()
                total += value * value
            norm = jnp.sqrt(jnp.sum(total)) + 1e-07
            for k, part in enumerate(parts):
                x[:, k * LANES : (k + 1) * LANES] = (part() / norm).astype(BF16)

        start(xq, [lambda k=k: chunks[k] for k in range(4)] + [lambda: low_half(chunks[4])])
        start(xk, [lambda: chunks[5], lambda: low_half(turn(chunks[4]))])
        start(xv, [lambda: chunks[6], lambda: low_half(chunks[7])])
        start(xo, [lambda k=k: chunks[8 + k] for k in range(4)] + [lambda: low_half(turn(chunks[7]))])

        def step(_, carry):
            wide_step(xq)
            wide_step(xo)
            tall_step(xk)
            tall_step(xv)
            return carry

        lax.fori_loop(0, 5, step, 0)

        def part(x, k):
            return x[:, k * LANES : (k + 1) * LANES].astype(F32)

        for k in range(4):
            chunks[k] = part(xq, k)
            chunks[8 + k] = part(xo, k)
        chunks[4] = join(part(xq, 4), turn(part(xk, 1)))
        chunks[5] = part(xk, 0)
        chunks[6] = part(xv, 0)
        chunks[7] = join(part(xv, 1), turn(part(xo, 4)))
        attention_lines_from_chunks(chunks, look)
        ortho_out[...] = look[...].astype(BF16)

    store_g.wait()
    store_m.wait()


def attention_update(scal, first, rest, state, grad_state, moment_state):
    lines = state.shape[0]
    return pl.pallas_call(
        attention_update_kernel,
        out_shape=(
            jax.ShapeDtypeStruct((lines, LANES), F32),
            jax.ShapeDtypeStruct((lines, LANES), F32),
            jax.ShapeDtypeStruct((PIECE_ROWS, LANES), BF16),
        ),
        in_specs=[SMEM_SPEC] + [VMEM_SPEC] * 16 + [ANY_SPEC] * 3,
        out_specs=(ANY_SPEC, ANY_SPEC, VMEM_SPEC),
        input_output_aliases={18: 0, 19: 1},
        scratch_shapes=[
            pltpu.VMEM((CHUNKS, D, LANES), F32),
            pltpu.VMEM((PIECE_ROWS, LANES), F32),
            pltpu.VMEM((PIECE_ROWS, LANES), F32),
            pltpu.VMEM((PIECE_ROWS, LANES), F32),
            pltpu.VMEM((D, 5 * LANES), BF16),
            pltpu.VMEM((D, 2 * LANES), BF16),
            pltpu.VMEM((D, 2 * LANES), BF16),
            pltpu.VMEM((D, 5 * LANES), BF16),
            pltpu.SemaphoreType.DMA((3,)),
        ],
        compiler_params=pltpu.CompilerParams(vmem_limit_bytes=VMEM_LIMIT),
        name="attention_update",
    )(scal, *first, *rest, state, grad_state, moment_state)


OUT_BAND = 1728


def weight_kernel(scal, state, ff_own, attn_own, received, out):
    core, half = scal[0], scal[2]
    in_ff = pl.program_id(0) // (PIECE_ROWS // OUT_BAND) == half
    mine = jnp.where(in_ff, ff_own[...].astype(F32), attn_own[...].astype(F32))
    ours = jnp.where(in_ff == (core == 0), mine, received[...].astype(F32))
    owned = jnp.where(in_ff, scal[3], scal[5]) != 0
    scale = jnp.where(in_ff, STEP_SCALE_FF, STEP_SCALE_ATTN)
    out[...] = jnp.where(owned, state[...] - scale * ours, state[...])


def weight_update(scal, state, ff_own, attn_own, received):
    lines = state.shape[0]
    bands = PIECE_ROWS // OUT_BAND
    whole = pl.BlockSpec((OUT_BAND, LANES), lambda i: (i, 0))
    piece = pl.BlockSpec((OUT_BAND, LANES), lambda i: (i % bands, 0))
    return pl.pallas_call(
        weight_kernel,
        out_shape=jax.ShapeDtypeStruct((lines, LANES), F32),
        grid=(lines // OUT_BAND,),
        in_specs=[SMEM_SPEC, whole, piece, piece, piece],
        out_specs=whole,
        compiler_params=pltpu.CompilerParams(vmem_limit_bytes=VMEM_LIMIT),
        name="weight_update",
    )(scal, state, ff_own, attn_own, received)


class Links:
    def __init__(self):
        self.rep, self.own, self.cp = (lax.axis_size(a) for a in ("rep", "own", "cp"))
        rep = lax.axis_index("rep")
        self.core = rep % 2
        self.quarter = 2 * ((rep // 2) % 2) + lax.axis_index("cp")
        self.plane = lax.axis_index("own")

    def partner(self, block):
        return lax.ppermute(block, "rep", [(i, i ^ 1) for i in range(self.rep)])

    def chip(self, block, step):
        flip = ((step & 2) * self.cp) | (step & 1)
        return lax.ppermute(block, ("rep", "cp"), [(i, i ^ flip) for i in range(self.rep * self.cp)])

    def beyond(self, total):
        far = 4
        while far < self.rep:
            total = total + lax.ppermute(total, "rep", [(i, i ^ far) for i in range(self.rep)])
            far *= 2
        return total

    def along(self, block, shift):
        return lax.ppermute(block, "own", [(i, (i + shift) % self.own) for i in range(self.own)])

    def spread(self, block):
        mine = [block] + [self.chip(block, step) for step in range(1, 4)]
        return mine + [self.partner(b) for b in mine]

    def plane_sum(self, grad):
        width = grad.shape[1] // 4
        other = lax.dynamic_slice_in_dim(grad, (1 - self.core) * HALF_ROWS, HALF_ROWS, 0)
        mine = lax.dynamic_slice_in_dim(grad, self.core * HALF_ROWS, HALF_ROWS, 0)
        both = mine + self.partner(other)

        def block(step):
            return lax.dynamic_slice_in_dim(both, (self.quarter ^ step) * width, width, 1)

        arrived = [self.chip(block(step), step) for step in range(1, 4)]
        total = sum((b.astype(F32) for b in arrived), block(0).astype(F32))
        return self.beyond(total.astype(BF16))

    def line_sum(self, block):
        arrived = [self.along(block, shift) for shift in range(1, self.own)]
        return sum((b.astype(F32) for b in arrived), block.astype(F32)).astype(BF16)

    def everywhere(self, value):
        for axis in ("rep", "cp", "own"):
            far = 1
            while far < lax.axis_size(axis):
                size = lax.axis_size(axis)
                value = value + lax.ppermute(value, axis, [(i, i ^ far) for i in range(size)])
                far *= 2
        return value


def per_device(
    tokens,
    cotangent,
    segment_ids,
    positions,
    assignment,
    weight_state,
    momentum_state,
    gains,
    gain_momentum,
):
    links = Links()
    part = lax.axis_index("cp")
    leader = assignment[0]
    leads = (links.plane == leader).astype(jnp.int32)
    owns_ff = jnp.any(assignment[4:] == links.plane).astype(jnp.int32)
    owns_down = (assignment[6] == links.plane).astype(jnp.int32)
    scal = jnp.stack([links.core, links.quarter, leads, owns_ff, owns_down, leads]).astype(jnp.int32)
    weight_lines = weight_state.reshape(-1, LANES)
    moment_lines = momentum_state.reshape(-1, LANES)

    def from_plane(block, owner):
        result = block
        for shift in range(1, links.own):
            result = jnp.where(links.plane == (owner + shift) % links.own, shifted[id(block)][shift], result)
        return result

    first = extract_first(scal, weight_lines)
    rest, ff_block = extract_rest(scal, weight_lines)
    shifted = {
        id(b): [b] + [links.along(b, shift) for shift in range(1, links.own)] for b in (first, rest, ff_block)
    }
    w_first = assemble(scal, links.spread(from_plane(first, leader)))
    w_rest = assemble(scal, links.spread(from_plane(rest, leader)))
    weight_gate, weight_up, weight_down_t = (
        assemble(scal, links.spread(from_plane(ff_block, assignment[m]))) for m in (4, 5, 6)
    )
    weight_q, weight_k, weight_v = w_first[:, :576], w_first[:, 576:768], w_first[:, 768:960]
    weight_o = jnp.concatenate([w_rest, w_first[:, 960:]], axis=1)
    half_len = tokens.shape[1]
    model_width = tokens.shape[2]
    share = HEADS // KV_HEADS
    block_count = half_len // QBLOCK
    item_count = block_count * KV_HEADS
    inputs = tokens[0].astype(jnp.float32)
    places = positions[0]
    segments = segment_ids[0]
    normed_one = rms_normalize(inputs, gains[0]).astype(jnp.bfloat16)
    queries = rotate(product(normed_one, weight_q), places, 1.0).astype(jnp.bfloat16)
    key_rows = rotate(product(normed_one, weight_k), places, 1.0).astype(jnp.bfloat16)
    value_rows = product(normed_one, weight_v).astype(jnp.bfloat16)
    segment_low = segments.astype(jnp.bfloat16)
    prior_keys, prior_values, prior_segments = from_behind(
        (key_rows, value_rows, segment_low), "cp", 1
    )
    all_keys = jnp.concatenate([prior_keys, key_rows], axis=0)
    all_values = jnp.concatenate([prior_values, value_rows], axis=0)
    key_segments = jnp.concatenate([prior_segments, segment_low], axis=0).astype(jnp.float32)
    key_groups = all_keys.reshape(2 * half_len, KV_HEADS, HEAD).transpose(1, 0, 2)
    value_groups = all_values.reshape(2 * half_len, KV_HEADS, HEAD).transpose(1, 0, 2)

    def to_items(array):
        shaped = array.reshape(block_count, QBLOCK, KV_HEADS, share * HEAD).transpose(0, 2, 1, 3)
        return shaped.reshape(item_count, QBLOCK, share, HEAD)

    def from_items(array):
        shaped = array.reshape(block_count, KV_HEADS, QBLOCK, share * HEAD).transpose(0, 2, 1, 3)
        return shaped.reshape(half_len, model_width)

    item_index = jnp.arange(item_count, dtype=jnp.int32)
    item_block = item_index // KV_HEADS
    item_group = item_index % KV_HEADS
    key_index = (part - 1) * half_len + jnp.arange(2 * half_len)

    def block_scores(block_queries, block, group):
        query_index = part * half_len + block * QBLOCK + jnp.arange(QBLOCK)
        query_segments = segments.astype(jnp.float32)
        allowed = (
            (key_index[None, :] <= query_index[:, None])
            & (key_index[None, :] >= 0)
            & (query_segments[:, None] == key_segments[None, :])
        )
        key_heads = key_groups[group]
        scores = jnp.einsum(
            "qrd,kd->rqk", block_queries, key_heads, preferred_element_type=jnp.float32
        ) * HEAD ** (-0.5)
        return (jnp.where(allowed[None], scores, -jnp.inf), key_heads)

    def forward_block(items):
        block_queries, block, group = items
        scores, key_heads = block_scores(block_queries, block, group)
        highest = jnp.max(scores, axis=-1, keepdims=True)
        log_total = highest + jnp.log(jnp.sum(jnp.exp(scores - highest), axis=-1, keepdims=True))
        attn_weights = jnp.exp(scores - log_total).astype(jnp.bfloat16)
        mixed_heads = jnp.einsum(
            "rqk,kd->qrd", attn_weights, value_groups[group], preferred_element_type=jnp.float32
        )
        return (mixed_heads.astype(jnp.bfloat16), log_total)

    query_items = to_items(queries)
    mixed_items, log_totals = lax.map(forward_block, (query_items, item_block, item_group))
    mixed_out = from_items(mixed_items)
    middle = inputs + product(mixed_out, weight_o)
    normed_two = rms_normalize(middle, gains[1]).astype(jnp.bfloat16)
    gate_proj = product(normed_two, weight_gate)
    up_proj = product(normed_two, weight_up)
    sigmoid_gate = jax.nn.sigmoid(gate_proj)
    silu_gate = gate_proj * sigmoid_gate
    hidden = (silu_gate * up_proj).astype(jnp.bfloat16)
    output = (middle + against(hidden, weight_down_t)).astype(jnp.bfloat16).reshape(tokens.shape)
    upstream = cotangent[0].astype(jnp.float32)
    low_upstream = upstream.astype(jnp.bfloat16)
    grad_down_t = over_rows(low_upstream, hidden)
    grad_hidden = product(low_upstream, weight_down_t)
    grad_gate = (
        grad_hidden * up_proj * sigmoid_gate * (1.0 + gate_proj * (1.0 - sigmoid_gate))
    ).astype(jnp.bfloat16)
    grad_up = (grad_hidden * silu_gate).astype(jnp.bfloat16)
    grad_gate_w = over_rows(normed_two, grad_gate)
    grad_up_w = over_rows(normed_two, grad_up)
    grad_normed_two = against(grad_gate, weight_gate) + against(grad_up, weight_up)
    back_two, gain_two_grad = norm_backward(middle, gains[1], grad_normed_two)
    grad_middle = upstream + back_two
    low_middle = grad_middle.astype(jnp.bfloat16)
    grad_out_w = over_rows(mixed_out, low_middle)
    grad_mixed = against(low_middle, weight_o).astype(jnp.bfloat16)

    def backward_block(items):
        block_queries, block, group, log_total, block_grad = items
        scores, key_heads = block_scores(block_queries, block, group)
        value_heads = value_groups[group]
        probabilities = jnp.exp(scores - log_total)
        attn_weights = probabilities.astype(jnp.bfloat16)
        grad_values = jnp.einsum(
            "rqk,qrd->kd", attn_weights, block_grad, preferred_element_type=jnp.float32
        )
        grad_weights = jnp.einsum(
            "qrd,kd->rqk", block_grad, value_heads, preferred_element_type=jnp.float32
        )
        row_dot = jnp.sum(probabilities * grad_weights, axis=-1, keepdims=True)
        grad_scores = (probabilities * (grad_weights - row_dot)).astype(jnp.bfloat16)
        grad_queries = jnp.einsum(
            "rqk,kd->qrd", grad_scores, key_heads, preferred_element_type=jnp.float32
        ) * HEAD ** (-0.5)
        grad_keys = jnp.einsum(
            "rqk,qrd->kd", grad_scores, block_queries, preferred_element_type=jnp.float32
        ) * HEAD ** (-0.5)
        return (grad_queries, grad_keys, grad_values)

    query_grads, key_items, value_items = lax.map(
        backward_block, (query_items, item_block, item_group, log_totals, to_items(grad_mixed))
    )

    def gather_groups(array):
        summed_blocks = jnp.sum(array.reshape(block_count, KV_HEADS, 2 * half_len, HEAD), axis=0)
        return summed_blocks.transpose(1, 0, 2).reshape(2 * half_len, KV_HEADS * HEAD)

    key_grads = gather_groups(key_items)
    value_grads = gather_groups(value_items)
    later_keys, later_values = from_behind((key_grads[:half_len], value_grads[:half_len]), "cp", -1)
    key_total = key_grads[half_len:] + later_keys
    value_total = value_grads[half_len:] + later_values
    grad_q = rotate(from_items(query_grads), places, -1.0).astype(jnp.bfloat16)
    grad_k = rotate(key_total, places, -1.0).astype(jnp.bfloat16)
    grad_v = value_total.astype(jnp.bfloat16)
    grad_q_w = over_rows(normed_one, grad_q)
    grad_k_w = over_rows(normed_one, grad_k)
    grad_v_w = over_rows(normed_one, grad_v)
    grad_normed_one = (
        against(grad_q, weight_q) + against(grad_k, weight_k) + against(grad_v, weight_v)
    )
    back_one, gain_one_grad = norm_backward(inputs, gains[0], grad_normed_one)
    input_grad = (grad_middle + back_one).reshape(tokens.shape)
    gain_local = jnp.stack([gain_one_grad, gain_two_grad])
    gain_grad = links.everywhere(gain_local)

    def low(grad):
        return links.plane_sum(grad.astype(BF16))

    down_sum, gate_sum, up_sum = low(grad_down_t), low(grad_gate_w), low(grad_up_w)
    rest_sum = low(grad_out_w[:, :512])
    first_sum = low(jnp.concatenate([grad_q_w, grad_k_w, grad_v_w, grad_out_w[:, 512:]], axis=1))

    def for_plane(plane):
        return jnp.where(
            assignment[4] == plane, gate_sum, jnp.where(assignment[5] == plane, up_sum, down_sum)
        )

    ff_sum = for_plane(links.plane).astype(F32)
    for shift in range(1, links.own):
        ff_sum += links.along(for_plane((links.plane + shift) % links.own), shift).astype(F32)
    ff_blocks = links.spread(ff_sum.astype(BF16))
    rest_blocks = links.spread(links.line_sum(rest_sum))
    first_blocks = links.spread(links.line_sum(first_sum))
    grad_state, moment_state, ff_ortho = ff_update(scal, ff_blocks, moment_lines)
    grad_state, moment_state, attn_ortho = attention_update(
        scal, first_blocks, rest_blocks, moment_lines, grad_state, moment_state
    )
    received = links.partner(jnp.where(links.core == 0, ff_ortho, attn_ortho))
    weight_next = weight_update(scal, weight_lines, ff_ortho, attn_ortho, received)
    gain_moment = MOMENTUM * gain_momentum + gain_grad
    push_gain = gain_grad + MOMENTUM * gain_moment
    gains_new = gains - GAIN_RATE * push_gain * lax.rsqrt(
        jnp.mean(push_gain * push_gain, axis=-1, keepdims=True) + 1e-06
    )
    return (
        output,
        input_grad,
        grad_state.reshape(weight_state.shape),
        weight_next.reshape(weight_state.shape),
        moment_state.reshape(weight_state.shape),
        gain_grad,
        gains_new,
        gain_moment,
    )


def solution(mesh):
    placed = (
        P(("rep", "own"), "cp", None),
        P(("rep", "own"), "cp", None),
        P(("rep", "own"), "cp"),
        P(("rep", "own"), "cp"),
        P(),
        P("own", None),
        P("own", None),
        P(),
        P(),
    )
    return jax.shard_map(
        per_device,
        mesh=mesh,
        in_specs=placed,
        out_specs=(
            P(("rep", "own"), "cp", None),
            P(("rep", "own"), "cp", None),
            P("own", None),
            P("own", None),
            P("own", None),
            P(),
            P(),
            P(),
        ),
        check_vma=False,
    )
```

```python
import functools
import math

import jax
import jax.numpy as jnp
from jax import lax
from jax.experimental import pallas as pl
from jax.experimental.pallas import tpu as pltpu
from jax.sharding import PartitionSpec as P

D = 576
HEADS = 9
KV_HEADS = 3
HEAD = 64
FF = 1536
SHARE = HEADS // KV_HEADS

EPSILON = 1e-05
MOMENTUM = 0.95
LEARN_RATE = 0.05
GAIN_RATE = 0.1
ROPE_BASE = 10000.0
QUINTIC_A = 3.4445
QUINTIC_B = -4.775
QUINTIC_C = 2.0315

F32 = jnp.float32
BF16 = jnp.bfloat16
LANES = 128
QUARTER = D // 4
PIECE_ROWS = D * FF // LANES
CHUNKS = FF // LANES
STEP_SCALE_FF = LEARN_RATE * 0.2 * math.sqrt(FF)
STEP_SCALE_ATTN = LEARN_RATE * 0.2 * math.sqrt(D)
VMEM_LIMIT = 60 << 20
VMEM_SPEC = pl.BlockSpec(memory_space=pltpu.VMEM)
SMEM_SPEC = pl.BlockSpec(memory_space=pltpu.SMEM)
ANY_SPEC = pl.BlockSpec(memory_space=pl.ANY)
Q_AT, K_AT, V_AT, O_AT = 0, 2592, 3456, 4320


def call(kernel, outs, in_specs, scratch=(), flops=0, nbytes=0, out_specs=None, aliases=None, grid=()):
    outs = tuple(jax.ShapeDtypeStruct(shape, dtype) for shape, dtype in outs)
    return pl.pallas_call(
        kernel,
        out_shape=outs,
        grid=grid,
        in_specs=in_specs,
        out_specs=out_specs or (VMEM_SPEC,) * len(outs),
        scratch_shapes=list(scratch),
        input_output_aliases=aliases or {},
        compiler_params=pltpu.CompilerParams(vmem_limit_bytes=VMEM_LIMIT),
        cost_estimate=pl.CostEstimate(flops=flops, bytes_accessed=nbytes, transcendentals=0),
    )


def product(left, right):
    return jnp.dot(left, right, preferred_element_type=F32)


def over_rows(left, right):
    return lax.dot_general(left, right, (((0,), (0,)), ((), ())), preferred_element_type=F32)


def against(left, right):
    return lax.dot_general(left, right, (((1,), (1,)), ((), ())), preferred_element_type=F32)


class Place:
    def __init__(self, assignment=None):
        rep = lax.axis_index("rep")
        self.core = rep % 2
        self.quarter = 2 * ((rep // 2) % 2) + lax.axis_index("cp")
        if assignment is not None:
            plane = lax.axis_index("own")
            self.leads = assignment[0] == plane
            self.owns_down = assignment[6] == plane
            self.owns_ff = (assignment[4] == plane) | (assignment[5] == plane) | self.owns_down
            self.ff_half = jnp.where(self.leads, 1, 0)


def tall_multiple(index, step):
    return pl.multiple_of(index * step, step)


def turn(value):
    return pltpu.roll(value, 64, 1)


def join(low, high):
    lane = lax.broadcasted_iota(jnp.int32, low.shape, 1)
    return jnp.where(lane < 64, low, high)


def rows_to_columns(take):
    even = [lambda k=k: take(k) for k in range(5)]
    odd = [lambda k=k: join(turn(take(4 + k)), turn(take(5 + k))) for k in range(4)]
    odd.append(lambda: turn(take(8)))
    return even, odd


def columns_to_rows(even, odd):
    lines = [lambda k=k: even(k) for k in range(4)]
    lines.append(lambda: join(even(4), turn(odd(0))))
    for k in range(1, 5):
        lines.append(lambda k=k: join(turn(odd(k - 1)), turn(odd(k))))
    return lines


def attention_chunks(q, k, v, o):
    even = [lambda i=i: q(i) for i in range(4)]
    even.append(lambda: join(q(4), turn(k(0))))
    even.append(lambda: join(turn(k(0)), turn(k(1))))
    even.append(lambda: v(0))
    even.append(lambda: join(v(1), turn(o(4))))
    even += [lambda i=i: o(i) for i in range(4)]
    odd = [lambda i=i: join(turn(q(4 + i)), turn(q(5 + i))) for i in range(4)]
    odd.append(lambda: join(turn(q(8)), k(1)))
    odd.append(lambda: k(2))
    odd.append(lambda: join(turn(v(1)), turn(v(2))))
    odd.append(lambda: join(turn(v(2)), o(8)))
    odd += [lambda i=i: join(turn(o(4 + i)), turn(o(5 + i))) for i in range(4)]
    return even, odd


def attention_lines(even, odd):
    q = columns_to_rows(even, odd)
    k = [
        lambda: join(turn(even(4)), turn(even(5))),
        lambda: join(turn(even(5)), odd(4)),
        lambda: odd(5),
    ]
    v = [
        lambda: even(6),
        lambda: join(even(7), turn(odd(6))),
        lambda: join(turn(odd(6)), turn(odd(7))),
    ]
    o = [lambda i=i: even(8 + i) for i in range(4)]
    o.append(lambda: join(turn(even(7)), turn(odd(8))))
    for i in range(1, 4):
        o.append(lambda i=i: join(turn(odd(7 + i)), turn(odd(8 + i))))
    o.append(lambda: join(turn(odd(11)), odd(7)))
    return q, k, v, o


def extract_first_kernel(state, out, qb, kb, vb, ob, mat, sems):
    here = Place()
    pairs = QUARTER // 2
    copies = []
    for n, (buf, at, lines) in enumerate(((qb, Q_AT, 648), (kb, K_AT, 216), (vb, V_AT, 216), (ob, O_AT, 648))):
        begin = pl.multiple_of(at + lines * here.quarter, 8)
        copies.append(pltpu.make_async_copy(state.at[pl.ds(begin, lines)], buf, sems.at[n]))
    for copy in copies:
        copy.start()
    for copy in copies:
        copy.wait()
    even, odd = attention_chunks(
        lambda i: qb[pl.ds(i, pairs, stride=9), :],
        lambda i: kb[pl.ds(i, pairs, stride=3), :],
        lambda i: vb[pl.ds(i, pairs, stride=3), :],
        lambda i: ob[pl.ds(i, pairs, stride=9), :],
    )
    for core in range(2):

        @pl.when(here.core == core)
        def _(core=core):
            for j in range(4):
                mat[pl.ds(0, pairs, stride=2), :] = even[4 * core + j]()
                mat[pl.ds(1, pairs, stride=2), :] = odd[4 * core + j]()
                out[:, j * LANES : (j + 1) * LANES] = mat[...].astype(BF16)


def extract_first(state):
    return call(
        extract_first_kernel,
        [((QUARTER, 4 * LANES), BF16)],
        [ANY_SPEC],
        [
            pltpu.VMEM((648, LANES), F32),
            pltpu.VMEM((216, LANES), F32),
            pltpu.VMEM((216, LANES), F32),
            pltpu.VMEM((648, LANES), F32),
            pltpu.VMEM((QUARTER, LANES), F32),
            pltpu.SemaphoreType.DMA((4,)),
        ],
        nbytes=1 << 20,
    )(state)[0]


def extract_rest_kernel(assignment, state, near_out, far_out, ob, fb, db, mat, cols, turned, sems):
    here = Place(assignment)
    pairs = QUARTER // 2
    base = here.ff_half * PIECE_ROWS
    copy_o = pltpu.make_async_copy(
        state.at[pl.ds(pl.multiple_of(O_AT + 648 * here.quarter, 8), 648)], ob, sems.at[0]
    )
    copy_o.start()
    outs = (near_out, far_out)

    @pl.when(jnp.logical_not(here.owns_down))
    def _():
        begin = pl.multiple_of(base + here.quarter * (PIECE_ROWS // 4), 8)
        copy = pltpu.make_async_copy(state.at[pl.ds(begin, PIECE_ROWS // 4)], fb, sems.at[1])
        copy.start()
        copy.wait()
        for core in range(2):

            @pl.when(here.core == core)
            def _(core=core):
                for half in range(2):
                    for j in range(3):
                        outs[half][:, j * LANES : (j + 1) * LANES] = fb[
                            pl.ds(6 * half + 3 * core + j, QUARTER, stride=CHUNKS), :
                        ].astype(BF16)

    @pl.when(here.owns_down)
    def _():
        copies = []
        for half in range(2):
            begin = pl.multiple_of(base + (2 * half + here.core) * (PIECE_ROWS // 4), 8)
            copies.append(
                pltpu.make_async_copy(state.at[pl.ds(begin, PIECE_ROWS // 4)], db.at[half], sems.at[1 + half])
            )
            copies[-1].start()
        for half in range(2):
            copies[half].wait()
            even, odd = rows_to_columns(lambda i: db[half, pl.ds(i, 192, stride=9), :])
            for k in range(5):
                cols[pl.ds(0, 192, stride=2), :] = even[k]()
                cols[pl.ds(1, 192, stride=2), :] = odd[k]()
                turned[k * LANES : (k + 1) * LANES, :] = cols[...].T
            outs[half][:, :384] = turned[pl.ds(tall_multiple(here.quarter, QUARTER), QUARTER), :].astype(BF16)

    copy_o.wait()
    even, odd = rows_to_columns(lambda i: ob[pl.ds(i, pairs, stride=9), :])
    for core in range(2):

        @pl.when(here.core == core)
        def _(core=core):
            for j in range(2):
                mat[pl.ds(0, pairs, stride=2), :] = even[2 * core + j]()
                mat[pl.ds(1, pairs, stride=2), :] = odd[2 * core + j]()
                near_out[:, (3 + j) * LANES : (4 + j) * LANES] = mat[...].astype(BF16)


def extract_rest(assignment, state):
    return call(
        extract_rest_kernel,
        [((QUARTER, 5 * LANES), BF16), ((QUARTER, 3 * LANES), BF16)],
        [SMEM_SPEC, ANY_SPEC],
        [
            pltpu.VMEM((648, LANES), F32),
            pltpu.VMEM((PIECE_ROWS // 4, LANES), F32),
            pltpu.VMEM((2, PIECE_ROWS // 4, LANES), F32),
            pltpu.VMEM((QUARTER, LANES), F32),
            pltpu.VMEM((FF // 4, LANES), F32),
            pltpu.VMEM((5 * LANES, FF // 4), F32),
            pltpu.SemaphoreType.DMA((3,)),
        ],
        nbytes=3 << 20,
    )(assignment, state)


def assemble_kernel(*refs):
    blocks, out, sems = refs[:4], refs[4], refs[5]
    quarter = Place().quarter
    copies = []
    for step in range(4):
        rows = pl.ds(tall_multiple(quarter ^ step, QUARTER), QUARTER)
        copies.append(pltpu.make_async_copy(blocks[step], out.at[rows], sems.at[step]))
        copies[-1].start()
    for copy in copies:
        copy.wait()


def assemble(blocks):
    width = blocks[0].shape[1]
    return call(
        assemble_kernel, [((D, width), BF16)], [ANY_SPEC] * 4, [pltpu.SemaphoreType.DMA((4,))], nbytes=4 * D * width
    )(*blocks)[0]


def rotated(value, cosine, sine):
    lane = lax.broadcasted_iota(jnp.int32, value.shape, 1)
    swapped = jnp.where(lane % HEAD < HEAD // 2, pltpu.roll(value, LANES - HEAD // 2, 1), pltpu.roll(value, HEAD // 2, 1))
    return value * cosine + swapped * sine


def inverse_norm(values):
    return lax.rsqrt(jnp.mean(values * values, axis=-1, keepdims=True) + EPSILON)


def chunk(k):
    return slice(k * LANES, (k + 1) * LANES)


def low_half(value):
    return join(value, jnp.zeros_like(value))


def begin_row(places):
    return lax.broadcasted_iota(jnp.int32, places.shape, 1) - places[...]


def reaches_back(places, part):
    half = places.shape[0] // 2
    return places[part * half] > part * half


def project_kernel(
    x_ref, gains, places, cosine, sine, mine, other,
    normed_out, q_out, k_out, v_out, kv_out, tail_out, begin_out, both,
):
    core = Place().core
    both[core] = mine[...]
    both[1 - core] = other[...]
    begin_out[...] = jnp.broadcast_to(begin_row(places).astype(F32), (LANES, places.shape[1])).T
    x = x_ref[...].astype(F32)
    normed = (x * inverse_norm(x) * gains[0:1, :]).astype(BF16)
    normed_out[...] = normed
    cos, sin = cosine[...], sine[...]
    low = product(normed, both[0])
    high = product(normed, both[1])
    turned = [rotated(low[:, chunk(k)], cos, sin) for k in range(4)]
    turned += [rotated(high[:, chunk(k)], cos, sin) for k in range(2)]
    for head in range(HEADS):
        value = turned[head // 2]
        q_out[head] = (low_half(turn(value) if head % 2 else value).astype(BF16).astype(F32) * HEAD**-0.5).astype(BF16)
    keys = [turn(turned[4]), turned[5], turn(turned[5])]
    values = [high[:, chunk(2)], turn(high[:, chunk(2)]), high[:, chunk(3)]]
    for group in range(KV_HEADS):
        k_out[group] = low_half(keys[group]).astype(BF16)
        v_out[group] = low_half(values[group]).astype(BF16)
    kv_out[:, chunk(0)] = join(keys[0], turn(keys[1])).astype(BF16)
    kv_out[:, chunk(1)] = join(keys[2], turn(values[0])).astype(BF16)
    kv_out[:, chunk(2)] = join(values[1], turn(values[2])).astype(BF16)
    tail_out[...] = low_half(turn(both[1, :, chunk(3)].astype(F32))).astype(BF16)


def project(x, gains, places, cosine, sine, mine, other):
    rows = x.shape[0]
    return call(
        project_kernel,
        [
            ((rows, D), BF16),
            ((HEADS, rows, LANES), BF16),
            ((KV_HEADS, rows, LANES), BF16),
            ((KV_HEADS, rows, LANES), BF16),
            ((rows, 2 * KV_HEADS * HEAD), BF16),
            ((D, LANES), BF16),
            ((rows, LANES), F32),
        ],
        [VMEM_SPEC] * 7,
        [pltpu.VMEM((2, D, 4 * LANES), BF16)],
        flops=2 * rows * D * 1024,
        nbytes=6 << 20,
    )(x, gains, places, cosine, sine, mine, other)


def attend_own_kernel(q, k, v, begin, top_out, sum_out, mixed_out, bias, mix_s):
    rows = q.shape[1]
    half = rows // 2
    query = lax.broadcasted_iota(jnp.int32, (rows, rows), 0)
    key = lax.broadcasted_iota(jnp.int32, (rows, rows), 1)
    bias[...] = jnp.where((key <= query) & (key.astype(F32) >= begin[:, :1]), 0.0, -jnp.inf)
    lane = lax.broadcasted_iota(jnp.int32, (half, LANES), 1)
    top_out[...] = jnp.zeros((rows, LANES), F32)
    sum_out[...] = jnp.ones((rows, LANES), F32)

    def group(g, _):
        for part in range(2):
            span = (part + 1) * half
            at = pl.ds(part * half, half)
            tops, sums = top_out[at, :], sum_out[at, :]
            for r in range(SHARE):
                head = g * SHARE + r
                scores = against(q[head, at, :], k[g, :span, :]) + bias[at, :span]
                top = jnp.max(scores, axis=1, keepdims=True)
                weights = jnp.exp(scores - top)
                total = jnp.sum(weights, axis=1, keepdims=True)
                mix_s[head, at, :] = product(weights.astype(BF16), v[g, :span, :]) / total
                tops = jnp.where(lane == head, top, tops)
                sums = jnp.where(lane == head, total, sums)
            top_out[at, :] = tops
            sum_out[at, :] = sums
        return 0

    lax.fori_loop(0, KV_HEADS, group, 0)
    for c in range(5):
        odd = turn(mix_s[2 * c + 1]) if c < 4 else jnp.zeros((rows, LANES), F32)
        mixed_out[:, chunk(c)] = join(mix_s[2 * c], odd)


def attend_own(q, k, v, begin):
    rows = q.shape[1]
    return call(
        attend_own_kernel,
        [((rows, LANES), F32), ((rows, LANES), F32), ((rows, 5 * LANES), F32)],
        [VMEM_SPEC] * 4,
        [pltpu.VMEM((rows, rows), F32), pltpu.VMEM((HEADS, rows, LANES), F32)],
        flops=8 * HEADS * rows * rows * LANES,
        nbytes=6 << 20,
    )(q, k, v, begin)


def heads_of(packed, k, v):
    parts = [packed[:, chunk(c)].astype(F32) for c in range(3)]
    for head in range(2 * KV_HEADS):
        value = parts[head // 2]
        target = k if head < KV_HEADS else v
        target[head % KV_HEADS] = low_half(turn(value) if head % 2 else value).astype(BF16)


def attend_prior_kernel(places, q, kv, begin, tops, sums, own, mixed_out, logs_out, k_out, v_out, bias, top_s, sum_s, mix_s, keep_s):
    rows = q.shape[1]
    half = rows // 2
    lane = lax.broadcasted_iota(jnp.int32, (half, LANES), 1)
    top_s[...] = tops[...]
    sum_s[...] = sums[...]

    @pl.when(reaches_back(places, 0))
    def _():
        heads_of(kv, k_out, v_out)
        key = lax.broadcasted_iota(jnp.int32, (rows, rows), 1) - rows
        bias[...] = jnp.where(key.astype(F32) >= begin[:, :1], 0.0, -jnp.inf)

    def finish(part, source):
        at = pl.ds(part * half, half)
        for c in range(4):
            mixed_out[at, chunk(c)] = source(at, c).astype(BF16)
        mixed_out[at, 4 * LANES : D] = source(at, 4)[:, :HEAD].astype(BF16)

    for part in range(2):
        at = pl.ds(part * half, half)

        @pl.when(jnp.logical_not(reaches_back(places, part)))
        def _():
            finish(part, lambda at, c: own[at, chunk(c)])

        @pl.when(reaches_back(places, part))
        def _():
            def group(g, _):
                old_tops, old_sums = top_s[at, :], sum_s[at, :]
                new_tops, new_sums = old_tops, old_sums
                for r in range(SHARE):
                    head = g * SHARE + r
                    here = lane == head
                    old_top = jnp.max(jnp.where(here, old_tops, -jnp.inf), axis=1, keepdims=True)
                    old_sum = jnp.max(jnp.where(here, old_sums, 0.0), axis=1, keepdims=True)
                    scores = against(q[head, at, :], k_out[g]) + bias[at, :]
                    top = jnp.maximum(old_top, jnp.max(scores, axis=1, keepdims=True))
                    weights = jnp.exp(scores - top)
                    kept = old_sum * jnp.exp(old_top - top)
                    total = kept + jnp.sum(weights, axis=1, keepdims=True)
                    mix_s[head, at, :] = product(weights.astype(BF16), v_out[g]) / total
                    keep_s[head, at, :] = jnp.broadcast_to(kept / total, (half, LANES))
                    new_tops = jnp.where(here, top, new_tops)
                    new_sums = jnp.where(here, total, new_sums)
                top_s[at, :] = new_tops
                sum_s[at, :] = new_sums
                return 0

            lax.fori_loop(0, KV_HEADS, group, 0)

            def merged(at, c):
                if c == 4:
                    return own[at, chunk(c)] * keep_s[8, at, :] + mix_s[8, at, :]
                keep = join(keep_s[2 * c, at, :], keep_s[2 * c + 1, at, :])
                return own[at, chunk(c)] * keep + join(mix_s[2 * c, at, :], turn(mix_s[2 * c + 1, at, :]))

            finish(part, merged)

    logs_out[...] = (top_s[...] + jnp.log(sum_s[...])).T[:16, :]


def attend_prior(places, q, kv, begin, tops, sums, own):
    rows = q.shape[1]
    return call(
        attend_prior_kernel,
        [((rows, D), BF16), ((16, rows), F32), ((KV_HEADS, rows, LANES), BF16), ((KV_HEADS, rows, LANES), BF16)],
        [SMEM_SPEC] + [VMEM_SPEC] * 6,
        [
            pltpu.VMEM((rows, rows), F32),
            pltpu.VMEM((rows, LANES), F32),
            pltpu.VMEM((rows, LANES), F32),
            pltpu.VMEM((HEADS, rows, LANES), F32),
            pltpu.VMEM((HEADS, rows, LANES), F32),
        ],
        flops=8 * HEADS * rows * rows * LANES,
        nbytes=8 << 20,
    )(places, q, kv, begin, tops, sums, own)


TRIO = 3 * (FF // 4)


def feed_half(normed, turned_normed, upstream, turned_upstream, mine, other, keep, send, out, back, scratch, first):
    gate_w, up_w, down_w, hidden_s, gate_s, up_s = scratch
    width = FF // 4
    rows = normed.shape[0]
    for j, w in enumerate((gate_w, up_w, down_w)):
        w[:, :width] = mine[:, j * width : (j + 1) * width]
        w[:, width:] = other[:, j * width : (j + 1) * width]
    step = rows // 2

    def part(i, _):
        at = pl.ds(pl.multiple_of(i * step, step), step)
        gate = product(normed[at, :], gate_w[...])
        up = product(normed[at, :], up_w[...])
        grad_hidden = product(upstream[at, :], down_w[...])
        sig = jax.nn.sigmoid(gate)
        silu = gate * sig
        hidden = (silu * up).astype(BF16)
        grad_gate = (grad_hidden * up * sig * (1.0 + gate * (1.0 - sig))).astype(BF16)
        grad_up = (grad_hidden * silu).astype(BF16)
        hidden_s[at, :] = hidden
        gate_s[at, :] = grad_gate
        up_s[at, :] = grad_up
        ahead = against(hidden, down_w[...])
        behind = against(grad_gate, gate_w[...]) + against(grad_up, up_w[...])
        if first:
            out[at, :] = ahead
            back[at, :] = behind
        else:
            out[at, :] += ahead
            back[at, :] += behind
        return 0

    lax.fori_loop(0, 2, part, 0)
    for j, (left, right) in enumerate(
        ((turned_normed, gate_s), (turned_normed, up_s), (turned_upstream, hidden_s))
    ):
        grad = product(left[...], right[...]).astype(BF16)
        keep[:, j * width : (j + 1) * width] = grad[:, :width]
        send[:, j * width : (j + 1) * width] = grad[:, width:]


FEED_SCRATCH = [pltpu.VMEM((D, FF // 2), BF16)] * 3


def feed_scratch(rows):
    return FEED_SCRATCH + [pltpu.VMEM((rows, FF // 2), BF16)] * 3


def feed_near_kernel(
    x, mixed, tail, turned_upstream, gains, mine, other,
    middle, normed, turned_normed, cotangent, w_out, out, back, keep, send,
    *scratch,
):
    core = Place().core
    for side, w in ((core, mine), (1 - core, other)):
        w_out[:, pl.ds(tall_multiple(side, 2 * LANES), 2 * LANES)] = w[:, TRIO : TRIO + 2 * LANES]
    w_out[:, 4 * LANES : D] = tail[:, :HEAD]
    value = x[...].astype(F32) + product(mixed[...], w_out[...])
    middle[...] = value
    low = value * inverse_norm(value) * gains[1:2, :]
    normed[...] = low.astype(BF16)
    turned_normed[...] = low.T.astype(BF16)
    cotangent[...] = turned_upstream[...].astype(F32).T.astype(BF16)
    feed_half(normed, turned_normed, cotangent, turned_upstream, mine, other, keep, send, out, back, scratch, True)


def feed_near(x, mixed, tail, turned_upstream, gains, mine, other):
    rows = x.shape[0]
    return call(
        feed_near_kernel,
        [
            ((rows, D), F32),
            ((rows, D), BF16),
            ((D, rows), BF16),
            ((rows, D), BF16),
            ((D, D), BF16),
            ((rows, D), F32),
            ((rows, D), F32),
            ((D, TRIO), BF16),
            ((D, TRIO), BF16),
        ],
        [VMEM_SPEC] * 7,
        feed_scratch(rows),
        flops=20 * rows * D * FF // 2,
        nbytes=16 << 20,
    )(x, mixed, tail, turned_upstream, gains, mine, other)


def feed_far_kernel(
    middle, normed, turned_normed, cotangent, turned_upstream, gains, mixed, w_out, out_in, back_in, mine, other,
    output, grad_middle_out, grad_mixed_out, dots_out, gain_out, tail_out, keep, send,
    out, back, *scratch,
):
    core = Place().core
    out[...] = out_in[...]
    back[...] = back_in[...]
    feed_half(
        normed, turned_normed, cotangent, turned_upstream, mine, other,
        keep.at[:, :TRIO], send.at[:, :TRIO], out, back, scratch, False,
    )
    value = middle[...]
    output[...] = (value + out[...]).astype(BF16)
    factor = inverse_norm(value)
    unit = value * factor
    upstream = back[...]
    gain_out[...] = jnp.sum(upstream * unit, axis=0, keepdims=True)
    scaled = upstream * gains[1:2, :]
    grad_middle = cotangent[...].astype(F32) + factor * (
        scaled - unit * jnp.mean(scaled * unit, axis=-1, keepdims=True)
    )
    grad_middle_out[...] = grad_middle
    low = grad_middle.astype(BF16)
    grad_w = product(mixed[...].astype(F32).T.astype(BF16), low)
    wide = 2 * LANES
    low_cols, high_cols = grad_w[:, :wide].astype(BF16), grad_w[:, wide : 2 * wide].astype(BF16)

    @pl.when(core == 0)
    def _():
        keep[:, TRIO:] = low_cols
        send[:, TRIO:] = high_cols

    @pl.when(core == 1)
    def _():
        keep[:, TRIO:] = high_cols
        send[:, TRIO:] = low_cols

    tail_out[:, :HEAD] = grad_w[:, 4 * LANES :]
    tail_out[:, HEAD:] = jnp.zeros((D, HEAD), F32)
    grad_mixed = against(low, w_out[...]).astype(BF16)
    wide_grad = grad_mixed.astype(F32)
    for head in range(HEADS):
        if head == HEADS - 1:
            grad_mixed_out[head, :, :HEAD] = grad_mixed[:, 4 * LANES :]
            grad_mixed_out[head, :, HEAD:] = jnp.zeros_like(grad_mixed[:, 4 * LANES :])
        else:
            part = wide_grad[:, chunk(head // 2)]
            grad_mixed_out[head] = low_half(turn(part) if head % 2 else part).astype(BF16)
    dots = (wide_grad * mixed[...].astype(F32)).T
    dots_out[...] = jnp.zeros_like(dots_out)
    for head in range(HEADS):
        dots_out[head : head + 1, :] = jnp.sum(dots[head * HEAD : (head + 1) * HEAD, :], axis=0, keepdims=True)


def feed_far(middle, normed, turned_normed, cotangent, turned_upstream, gains, mixed, w_out, out, back, mine, other):
    rows = middle.shape[0]
    return call(
        feed_far_kernel,
        [
            ((rows, D), BF16),
            ((rows, D), F32),
            ((HEADS, rows, LANES), BF16),
            ((16, rows), F32),
            ((1, D), F32),
            ((D, LANES), F32),
            ((D, TRIO + 2 * LANES), BF16),
            ((D, TRIO + 2 * LANES), BF16),
        ],
        [VMEM_SPEC] * 12,
        [pltpu.VMEM((rows, D), F32)] * 2 + feed_scratch(rows),
        flops=20 * rows * D * FF // 2,
        nbytes=16 << 20,
    )(middle, normed, turned_normed, cotangent, turned_upstream, gains, mixed, w_out, out, back, mine, other)


def head_back(head, g, keys, cols, q, k, v, grad_mixed, logs, dots, bias, key_acc, value_acc, query_acc):
    queries = q[head, cols, :]
    grads = grad_mixed[head, cols, :]
    scores = against(k[g, keys, :], queries) + bias[keys, cols]
    weights = jnp.exp(scores - logs[pl.ds(head, 1), cols])
    grad_weights = against(v[g, keys, :], grads)
    grad_scores = (weights * (grad_weights - dots[pl.ds(head, 1), cols])).astype(BF16)
    value_acc[g, keys, :] += product(weights.astype(BF16), grads)
    key_acc[g, keys, :] += product(grad_scores, queries)
    query_acc[head, :, cols] += over_rows(k[g, keys, :], grad_scores)[:HEAD, :]


def clear(*refs):
    for ref in refs:
        ref[...] = jnp.zeros_like(ref)


def back_prior_kernel(places, q, k, v, grad_mixed, logs, dots, places_row, kv_out, query_acc, bias, key_acc, value_acc):
    rows = q.shape[1]
    half = rows // 2
    clear(kv_out, query_acc)

    @pl.when(reaches_back(places, 0))
    def _():
        clear(key_acc, value_acc)
        key = lax.broadcasted_iota(jnp.int32, (rows, rows), 0) - rows
        bias[...] = jnp.where(key >= begin_row(places_row), 0.0, -jnp.inf)

        def group(g, _):
            for part in range(2):

                @pl.when(reaches_back(places, part))
                def _():
                    for r in range(SHARE):
                        head_back(
                            g * SHARE + r, g, slice(0, rows), slice(part * half, (part + 1) * half),
                            q, k, v, grad_mixed, logs, dots, bias, key_acc, value_acc, query_acc,
                        )

            return 0

        lax.fori_loop(0, KV_HEADS, group, 0)
        pack_back(key_acc, value_acc, kv_out)


def pack_back(key_acc, value_acc, out):
    parts = [acc[g] for acc in (key_acc, value_acc) for g in range(KV_HEADS)]
    for c in range(3):
        out[:, chunk(c)] = join(parts[2 * c], turn(parts[2 * c + 1])).astype(out.dtype)


def back_prior(places, q, k, v, grad_mixed, logs, dots, places_row):
    rows = q.shape[1]
    return call(
        back_prior_kernel,
        [((rows, 2 * KV_HEADS * HEAD), BF16), ((HEADS, HEAD, rows), F32)],
        [SMEM_SPEC] + [VMEM_SPEC] * 7,
        [
            pltpu.VMEM((rows, rows), F32),
            pltpu.VMEM((KV_HEADS, rows, LANES), F32),
            pltpu.VMEM((KV_HEADS, rows, LANES), F32),
        ],
        flops=20 * HEADS * rows * rows * LANES,
        nbytes=8 << 20,
    )(places, q, k, v, grad_mixed, logs, dots, places_row)


def back_own_kernel(q, k, v, grad_mixed, logs, dots, places_row, query_in, kv_out, query_acc, bias, key_acc, value_acc):
    rows = q.shape[1]
    half = rows // 2
    query_acc[...] = query_in[...]
    clear(key_acc, value_acc)
    key = lax.broadcasted_iota(jnp.int32, (rows, rows), 0)
    query = lax.broadcasted_iota(jnp.int32, (rows, rows), 1)
    bias[...] = jnp.where((key <= query) & (key >= begin_row(places_row)), 0.0, -jnp.inf)

    def group(g, _):
        for r in range(SHARE):
            for part in range(2):
                head_back(
                    g * SHARE + r, g, slice(part * half, (part + 1) * half), slice(part * half, rows),
                    q, k, v, grad_mixed, logs, dots, bias, key_acc, value_acc, query_acc,
                )
        return 0

    lax.fori_loop(0, KV_HEADS, group, 0)
    pack_back(key_acc, value_acc, kv_out)


def back_own(q, k, v, grad_mixed, logs, dots, places_row, query_part):
    rows = q.shape[1]
    return call(
        back_own_kernel,
        [((rows, 2 * KV_HEADS * HEAD), F32), ((HEADS, HEAD, rows), F32)],
        [VMEM_SPEC] * 8,
        [
            pltpu.VMEM((rows, rows), F32),
            pltpu.VMEM((KV_HEADS, rows, LANES), F32),
            pltpu.VMEM((KV_HEADS, rows, LANES), F32),
        ],
        flops=20 * HEADS * rows * rows * LANES,
        nbytes=8 << 20,
    )(q, k, v, grad_mixed, logs, dots, places_row, query_part)


def first_grads_kernel(kv, kv_later, query_grad, cosine, sine, normed, tail, keep, send, packed_out, flat):
    core = Place().core
    rows = normed.shape[0]
    cos, sin = cosine[...], -sine[...]
    for head in range(HEADS):
        flat[head * HEAD : (head + 1) * HEAD, :] = query_grad[head] * HEAD**-0.5
    flat[HEADS * HEAD :, :] = jnp.zeros((HEAD, rows), F32)
    parts = [kv[:, chunk(c)] + kv_later[:, chunk(c)].astype(F32) for c in range(3)]
    chunks = [flat[chunk(c), :].T for c in range(5)]
    chunks[4] = join(chunks[4], turn(parts[0]))
    chunks.append(join(turn(parts[0]), turn(parts[1])))
    chunks.append(join(turn(parts[1]), turn(parts[2])))
    chunks.append(low_half(turn(parts[2])))
    for c in range(8):
        value = rotated(chunks[c], cos, sin) if c < 6 else chunks[c]
        packed_out[:, chunk(c)] = value.astype(BF16)
    turned = normed[...].astype(F32).T.astype(BF16)
    wide = 4 * LANES
    low = product(turned, packed_out[:, :wide]).astype(BF16)
    high = product(turned, packed_out[:, wide:])
    last = join(high[:, chunk(3)], turn(tail[...])).astype(BF16)

    def store(ref):
        ref[:, : 3 * LANES] = high[:, : 3 * LANES].astype(BF16)
        ref[:, 3 * LANES :] = last

    @pl.when(core == 0)
    def _():
        keep[...] = low
        store(send)

    @pl.when(core == 1)
    def _():
        send[...] = low
        store(keep)


def first_grads(kv, kv_later, query_grad, cosine, sine, normed, tail):
    rows = normed.shape[0]
    return call(
        first_grads_kernel,
        [((D, 4 * LANES), BF16), ((D, 4 * LANES), BF16), ((rows, 8 * LANES), BF16)],
        [VMEM_SPEC] * 7,
        [pltpu.VMEM((5 * LANES, rows), F32)],
        flops=2 * rows * D * 1024,
        nbytes=6 << 20,
    )(kv, kv_later, query_grad, cosine, sine, normed, tail)


def input_grad_kernel(x_ref, gains, packed, mine, other, grad_middle, output, out, output_out, gain_out, both):
    core = Place().core
    both[core] = mine[...]
    both[1 - core] = other[...]
    wide = 4 * LANES
    upstream = against(packed[:, :wide], both[0]) + against(packed[:, wide:], both[1])
    x = x_ref[...].astype(F32)
    factor = inverse_norm(x)
    unit = x * factor
    gain_out[...] = jnp.sum(upstream * unit, axis=0, keepdims=True)
    scaled = upstream * gains[0:1, :]
    total = grad_middle[...] + factor * (scaled - unit * jnp.mean(scaled * unit, axis=-1, keepdims=True))
    out[...] = total.T
    output_out[...] = output[...].astype(F32).T.astype(BF16)


def input_grad_of(x, gains, packed, mine, other, grad_middle, output):
    rows = x.shape[0]
    return call(
        input_grad_kernel,
        [((D, rows), F32), ((D, rows), BF16), ((1, D), F32)],
        [VMEM_SPEC] * 7,
        [pltpu.VMEM((2, D, 4 * LANES), BF16)],
        flops=2 * rows * D * 1024,
        nbytes=6 << 20,
    )(x, gains, packed, mine, other, grad_middle, output)


def quintic(square):
    return (
        QUINTIC_B * square.astype(F32)
        + QUINTIC_C * jnp.dot(square, square, preferred_element_type=F32)
    ).astype(BF16)


def wide_step(x_ref):
    x = x_ref[...]
    mixer = quintic(against(x, x).astype(BF16))
    x_ref[...] = (QUINTIC_A * x.astype(F32) + product(mixer, x)).astype(BF16)


def tall_step(x_ref):
    x = x_ref[...]
    mixer = quintic(over_rows(x, x).astype(BF16))
    x_ref[...] = (QUINTIC_A * x.astype(F32) + against(x, mixer)).astype(BF16)


BAND = 864


def momentum_pass(grad, moment):
    def band(i, _):
        rows = pl.ds(pl.multiple_of(i * BAND, BAND), BAND)
        moment[rows, :] = MOMENTUM * moment[rows, :] + grad[rows, :]
        return 0

    lax.fori_loop(0, PIECE_ROWS // BAND, band, 0)


def ff_lines_from_chunks(is_down, chunks, columns, lines):
    @pl.when(is_down == 0)
    def _():
        for k in range(CHUNKS):
            lines[pl.ds(k, D, stride=CHUNKS), :] = chunks[k]

    @pl.when(is_down != 0)
    def _():
        for k in range(CHUNKS):
            tall = chunks[k].T
            for j in range(5):
                width = min(LANES, D - j * LANES)
                columns[j, k * LANES : (k + 1) * LANES, :width] = tall[:, j * LANES : j * LANES + width]
        half = FF // 2
        getters = columns_to_rows(
            lambda j: columns[j, pl.ds(0, half, stride=2), :],
            lambda j: columns[j, pl.ds(1, half, stride=2), :],
        )
        for k in range(9):
            lines[pl.ds(k, half, stride=9), :] = getters[k]()


def attention_lines_from_chunks(chunks, lines):
    pairs = D // 2
    parts = attention_lines(
        lambda j: chunks[j, pl.ds(0, pairs, stride=2), :],
        lambda j: chunks[j, pl.ds(1, pairs, stride=2), :],
    )
    for begin, getters in zip((Q_AT, K_AT, V_AT, O_AT), parts):
        for k, getter in enumerate(getters):
            lines[pl.ds(begin + k, pairs, stride=len(getters)), :] = getter()


def gather_chunks(chunks, parts):
    for block, at in parts:
        for k in range(block.shape[1] // LANES):
            chunks[at + k] = block[:, k * LANES : (k + 1) * LANES].astype(F32)


def prepare_kernel(assignment, weights, moments, weight_out, moment_out, grad_out, wb, mb, zeros, sems):
    here = Place(assignment)
    zeros[...] = jnp.zeros_like(zeros)
    for owned, half in ((here.owns_ff, here.ff_half), (here.leads, 1 - here.ff_half)):

        @pl.when(jnp.logical_not(owned))
        def _():
            rows = pl.ds(pl.multiple_of(half * PIECE_ROWS, 8), PIECE_ROWS)
            loads = [
                pltpu.make_async_copy(source.at[rows], buf, sems.at[n])
                for n, (source, buf) in enumerate(((weights, wb), (moments, mb)))
            ]
            stores = [
                pltpu.make_async_copy(buf, target.at[rows], sems.at[2 + n])
                for n, (buf, target) in enumerate(((wb, weight_out), (mb, moment_out), (zeros, grad_out)))
            ]
            loads[0].start()
            loads[1].start()
            stores[2].start()
            loads[0].wait()
            stores[0].start()
            loads[1].wait()
            stores[1].start()
            for store in stores:
                store.wait()


def prepare(assignment, weights, moments):
    shape = (weights.shape, F32)
    buf = pltpu.VMEM((PIECE_ROWS, LANES), F32)
    return call(
        prepare_kernel,
        [shape] * 3,
        [SMEM_SPEC, ANY_SPEC, ANY_SPEC],
        [buf, buf, buf, pltpu.SemaphoreType.DMA((5,))],
        nbytes=20 << 20,
        out_specs=(ANY_SPEC,) * 3,
    )(assignment, weights, moments)


LINES_SCRATCH = pltpu.VMEM((PIECE_ROWS, LANES), F32)


def piece_lines(half):
    return pl.ds(pl.multiple_of(half * PIECE_ROWS, 8), PIECE_ROWS)


def add_momentum(rows, fetch, grad, moment, grad_out, moment_out, sems):
    fetch.wait()
    momentum_pass(grad, moment)
    stores = [
        pltpu.make_async_copy(grad, grad_out.at[rows], sems.at[1]),
        pltpu.make_async_copy(moment, moment_out.at[rows], sems.at[2]),
    ]
    for store in stores:
        store.start()
    for store in stores:
        store.wait()


def ff_lines_kernel(assignment, near, near_other, far, far_other, state, _grad, _moment, grad_out, moment_out,
                    chunks, grad, moment, columns, sems):
    here = Place(assignment)

    @pl.when(here.owns_ff)
    def _():
        rows = piece_lines(here.ff_half)
        fetch = pltpu.make_async_copy(state.at[rows], moment, sems.at[0])
        fetch.start()
        mine, theirs = 3 * here.core, 3 * (1 - here.core)
        width = 3 * LANES
        gather_chunks(
            chunks,
            [
                (near, mine),
                (near_other, theirs),
                (far.at[:, :width], 6 + mine),
                (far_other.at[:, :width], 6 + theirs),
            ],
        )
        ff_lines_from_chunks(jnp.where(here.owns_down, 1, 0), chunks, columns, grad)
        add_momentum(rows, fetch, grad, moment, grad_out, moment_out, sems)


def lines_outs(state):
    return [(state.shape, F32), (state.shape, F32)]


def ff_lines(assignment, near, near_other, far, far_other, state, grad_state, moment_state):
    return call(
        ff_lines_kernel,
        lines_outs(state),
        [SMEM_SPEC] + [VMEM_SPEC] * 4 + [ANY_SPEC] * 3,
        [
            pltpu.VMEM((CHUNKS, D, LANES), F32),
            LINES_SCRATCH,
            LINES_SCRATCH,
            pltpu.VMEM((5, FF, LANES), F32),
            pltpu.SemaphoreType.DMA((3,)),
        ],
        nbytes=14 << 20,
        out_specs=(ANY_SPEC,) * 2,
        aliases={6: 0, 7: 1},
    )(assignment, near, near_other, far, far_other, state, grad_state, moment_state)


def attention_lines_kernel(assignment, first, first_other, rest, rest_other, state, _grad, _moment, grad_out, moment_out,
                           chunks, grad, moment, sems):
    here = Place(assignment)

    @pl.when(here.leads)
    def _():
        rows = piece_lines(1 - here.ff_half)
        fetch = pltpu.make_async_copy(state.at[rows], moment, sems.at[0])
        fetch.start()
        core, other = here.core, 1 - here.core
        gather_chunks(
            chunks,
            [
                (first, 4 * core),
                (first_other, 4 * other),
                (rest.at[:, 3 * LANES :], 8 + 2 * core),
                (rest_other.at[:, 3 * LANES :], 8 + 2 * other),
            ],
        )
        attention_lines_from_chunks(chunks, grad)
        add_momentum(rows, fetch, grad, moment, grad_out, moment_out, sems)


def attention_lines_update(assignment, first, first_other, rest, rest_other, state, grad_state, moment_state):
    return call(
        attention_lines_kernel,
        lines_outs(state),
        [SMEM_SPEC] + [VMEM_SPEC] * 4 + [ANY_SPEC] * 3,
        [pltpu.VMEM((CHUNKS, D, LANES), F32), LINES_SCRATCH, LINES_SCRATCH, pltpu.SemaphoreType.DMA((3,))],
        nbytes=14 << 20,
        out_specs=(ANY_SPEC,) * 2,
        aliases={6: 0, 7: 1},
    )(assignment, first, first_other, rest, rest_other, state, grad_state, moment_state)


def ortho_kernel(assignment, grad_state, moment_state, out, chunks, grad, moment, columns, x, xq, xk, xv, xo, low, sems):
    here = Place(assignment)
    is_ff = here.core == 0

    @pl.when(jnp.where(is_ff, here.owns_ff, here.leads))
    def _():
        rows = piece_lines(jnp.where(is_ff, here.ff_half, 1 - here.ff_half))
        fetches = [
            pltpu.make_async_copy(source.at[rows], buf, sems.at[n])
            for n, (source, buf) in enumerate(((grad_state, grad), (moment_state, moment)))
        ]
        for fetch in fetches:
            fetch.start()
        for fetch in fetches:
            fetch.wait()

        @pl.when(is_ff)
        def _():
            ff_ortho(jnp.where(here.owns_down, 1, 0), chunks, grad, moment, columns, x)

        @pl.when(jnp.logical_not(is_ff))
        def _():
            attention_ortho(chunks, grad, moment, xq, xk, xv, xo)

        low[...] = grad[...].astype(BF16)
        store = pltpu.make_async_copy(low, out, sems.at[0])
        store.start()
        store.wait()


def orthogonalize(assignment, grad_state, moment_state):
    return call(
        ortho_kernel,
        [((PIECE_ROWS, LANES), BF16)],
        [SMEM_SPEC, ANY_SPEC, ANY_SPEC],
        [
            pltpu.VMEM((CHUNKS, D, LANES), F32),
            LINES_SCRATCH,
            LINES_SCRATCH,
            pltpu.VMEM((5, FF, LANES), F32),
            pltpu.VMEM((D, FF), BF16),
            pltpu.VMEM((D, 5 * LANES), BF16),
            pltpu.VMEM((D, 2 * LANES), BF16),
            pltpu.VMEM((D, 2 * LANES), BF16),
            pltpu.VMEM((D, 5 * LANES), BF16),
            pltpu.VMEM((PIECE_ROWS, LANES), BF16),
            pltpu.SemaphoreType.DMA((2,)),
        ],
        flops=12 * 10**9,
        nbytes=10 << 20,
        out_specs=(ANY_SPEC,),
    )(assignment, grad_state, moment_state)[0]


def ff_ortho(is_down, chunks, grad, moment, columns, x):
    def ahead(lines):
        return grad[lines, :] + MOMENTUM * moment[lines, :]

    @pl.when(is_down == 0)
    def _():
        for k in range(CHUNKS):
            chunks[k] = ahead(pl.ds(k, D, stride=CHUNKS))

    @pl.when(is_down != 0)
    def _():
        even, odd = rows_to_columns(lambda i: ahead(pl.ds(i, FF // 2, stride=9)))
        for j in range(5):
            columns[j, pl.ds(0, FF // 2, stride=2), :] = even[j]()
            columns[j, pl.ds(1, FF // 2, stride=2), :] = odd[j]()
            width = min(LANES, D - j * LANES)
            for k in range(CHUNKS):
                tall = columns[j, k * LANES : (k + 1) * LANES, :].T
                chunks[k, j * LANES : j * LANES + width, :] = tall[:width, :]

    total = jnp.zeros((D, LANES), F32)
    for k in range(CHUNKS):
        total += chunks[k] * chunks[k]
    norm = jnp.sqrt(jnp.sum(total)) + 1e-07
    for k in range(CHUNKS):
        x[:, k * LANES : (k + 1) * LANES] = (chunks[k] / norm).astype(BF16)

    def step(_, carry):
        wide_step(x)
        return carry

    lax.fori_loop(0, 5, step, 0)
    for k in range(CHUNKS):
        chunks[k] = x[:, k * LANES : (k + 1) * LANES].astype(F32)
    ff_lines_from_chunks(is_down, chunks, columns, grad)


def attention_ortho(chunks, grad, moment, xq, xk, xv, xo):
    pairs = D // 2

    def ahead(begin, stride):
        def take(i):
            lines = pl.ds(begin + i, pairs, stride=stride)
            return grad[lines, :] + MOMENTUM * moment[lines, :]

        return take

    even, odd = attention_chunks(ahead(Q_AT, 9), ahead(K_AT, 3), ahead(V_AT, 3), ahead(O_AT, 9))
    for k in range(CHUNKS):
        chunks[k, pl.ds(0, pairs, stride=2), :] = even[k]()
        chunks[k, pl.ds(1, pairs, stride=2), :] = odd[k]()

    def start(x, parts):
        total = jnp.zeros((D, LANES), F32)
        for part in parts:
            value = part()
            total += value * value
        norm = jnp.sqrt(jnp.sum(total)) + 1e-07
        for k, part in enumerate(parts):
            x[:, k * LANES : (k + 1) * LANES] = (part() / norm).astype(BF16)

    start(xq, [lambda k=k: chunks[k] for k in range(4)] + [lambda: low_half(chunks[4])])
    start(xk, [lambda: chunks[5], lambda: low_half(turn(chunks[4]))])
    start(xv, [lambda: chunks[6], lambda: low_half(chunks[7])])
    start(xo, [lambda k=k: chunks[8 + k] for k in range(4)] + [lambda: low_half(turn(chunks[7]))])

    def step(_, carry):
        wide_step(xq)
        wide_step(xo)
        tall_step(xk)
        tall_step(xv)
        return carry

    lax.fori_loop(0, 5, step, 0)

    def part(x, k):
        return x[:, k * LANES : (k + 1) * LANES].astype(F32)

    for k in range(4):
        chunks[k] = part(xq, k)
        chunks[8 + k] = part(xo, k)
    chunks[4] = join(part(xq, 4), turn(part(xk, 1)))
    chunks[5] = part(xk, 0)
    chunks[6] = part(xv, 0)
    chunks[7] = join(part(xv, 1), turn(part(xo, 4)))
    attention_lines_from_chunks(chunks, grad)


BANDS = 4


def weight_kernel(side, assignment, state, ortho, _weights, out, wb, ob, sems):
    here = Place(assignment)
    is_ff = here.core == side
    half = jnp.where(is_ff, here.ff_half, 1 - here.ff_half)
    scale = jnp.where(is_ff, STEP_SCALE_FF, STEP_SCALE_ATTN)

    @pl.when(jnp.where(is_ff, here.owns_ff, here.leads))
    def _():
        size = PIECE_ROWS // BANDS
        stores = []
        loads = []
        for band in range(BANDS):
            rows = pl.ds(band * size, size)
            place = pl.ds(pl.multiple_of(half * PIECE_ROWS + band * size, 8), size)
            loads.append(
                (
                    pltpu.make_async_copy(state.at[place], wb.at[rows], sems.at[0, band]),
                    pltpu.make_async_copy(ortho.at[rows], ob.at[rows], sems.at[1, band]),
                )
            )
            stores.append(pltpu.make_async_copy(wb.at[rows], out.at[place], sems.at[2, band]))
        for pair in loads:
            for copy in pair:
                copy.start()
        for band in range(BANDS):
            rows = pl.ds(band * size, size)
            for copy in loads[band]:
                copy.wait()
            wb[rows, :] = wb[rows, :] - scale * ob[rows, :].astype(F32)
            stores[band].start()
        for store in stores:
            store.wait()


def weight_update(side, assignment, state, ortho, weights):
    return call(
        functools.partial(weight_kernel, side),
        [(state.shape, F32)],
        [SMEM_SPEC, ANY_SPEC, ANY_SPEC, ANY_SPEC],
        [LINES_SCRATCH, pltpu.VMEM((PIECE_ROWS, LANES), BF16), pltpu.SemaphoreType.DMA((3, BANDS))],
        nbytes=9 << 20,
        out_specs=(ANY_SPEC,),
        aliases={3: 0},
    )(assignment, state, ortho, weights)[0]


def split_sum_kernel(keep, arrived, *outs):
    quarter = Place().quarter
    for step in range(4):
        rows = pl.ds(tall_multiple(quarter ^ step, QUARTER), QUARTER)
        outs[step][...] = (keep[rows, :].astype(F32) + arrived[rows, :].astype(F32)).astype(BF16)


def split_sum(keep, arrived):
    width = keep.shape[1]
    return call(split_sum_kernel, [((QUARTER, width), BF16)] * 4, [VMEM_SPEC] * 2, nbytes=6 * D * width)(keep, arrived)


def by_plane_kernel(planes, assignment, *refs):
    count = len(refs) - planes - 1
    blocks, outs, total = refs[:count], refs[count:-1], refs[-1]
    value = blocks[0][...].astype(F32)
    for block in blocks[1:]:
        value += block[...].astype(F32)
    total[...] = value.astype(BF16)
    width = FF // 4
    for shift in range(planes):
        plane = lax.rem(lax.axis_index("own") + shift, planes)
        piece = jnp.where(assignment[5] == plane, 1, jnp.where(assignment[6] == plane, 2, 0))
        outs[shift][:, :width] = total[:, pl.ds(tall_multiple(piece, width), width)]
        if outs[shift].shape[1] > width:
            outs[shift][:, width:] = total[:, TRIO:]


def by_plane(planes, assignment, blocks):
    width = blocks[0].shape[1]
    return call(
        functools.partial(by_plane_kernel, planes),
        [((QUARTER, width - 2 * (FF // 4)), BF16)] * planes,
        [SMEM_SPEC] + [VMEM_SPEC] * len(blocks),
        [pltpu.VMEM((QUARTER, width), BF16)],
        nbytes=12 * QUARTER * width,
    )(assignment, *blocks)


def pick_kernel(assignment, *refs):
    line, out = refs[:-1], refs[-1]
    planes = len(line)
    width = FF // 4

    def pick(owner, columns):
        shift = lax.rem(lax.axis_index("own") - owner + planes, planes)
        value = line[0][:, columns]
        for n in range(1, planes):
            value = jnp.where(shift == n, line[n][:, columns], value)
        return value

    for j in range(3):
        out[:, j * width : (j + 1) * width] = pick(assignment[4 + j], slice(0, width))
    if out.shape[1] > TRIO:
        out[:, TRIO:] = pick(assignment[0], slice(width, line[0].shape[1]))


def pick_pieces(assignment, line):
    width = TRIO + line[0].shape[1] - FF // 4
    return call(
        pick_kernel, [((QUARTER, width), BF16)], [SMEM_SPEC] + [VMEM_SPEC] * len(line), nbytes=4 << 20
    )(assignment, *line)[0]


def total(blocks):
    return sum((b.astype(F32) for b in blocks[1:]), blocks[0].astype(F32)).astype(BF16)


class Links:
    def __init__(self):
        self.rep, self.own, self.cp = (lax.axis_size(a) for a in ("rep", "own", "cp"))
        self.quarter = Place().quarter
        self.plane = lax.axis_index("own")

    def partner(self, block):
        return lax.ppermute(block, "rep", [(i, i ^ 1) for i in range(self.rep)])

    def chip(self, block, step):
        flip = ((step & 2) * self.cp) | (step & 1)
        return lax.ppermute(block, ("rep", "cp"), [(i, i ^ flip) for i in range(self.rep * self.cp)])

    def beyond(self, total):
        far = 4
        while far < self.rep:
            total = total + lax.ppermute(total, "rep", [(i, i ^ far) for i in range(self.rep)])
            far *= 2
        return total

    def along(self, block, shift):
        return lax.ppermute(block, "own", [(i, (i + shift) % self.own) for i in range(self.own)])

    def line(self, block):
        return [block] + [self.along(block, shift) for shift in range(1, self.own)]

    def pick(self, arrived, owner):
        block = arrived[0]
        for shift in range(1, self.own):
            block = jnp.where(self.plane == (owner + shift) % self.own, arrived[shift], block)
        return block

    def spread(self, block):
        blocks = [block] + [self.chip(block, step) for step in range(1, 4)]
        mine = assemble(blocks)
        return mine, self.partner(mine)

    def plane_parts(self, keep, send):
        arrived = self.partner(send)
        blocks = split_sum(keep, arrived)
        blocks = [blocks[0]] + [self.chip(blocks[step], step) for step in range(1, 4)]
        if self.rep > 4:
            blocks = [self.beyond(total(blocks))]
        return blocks

    def line_sum(self, blocks):
        blocks = [blocks[0]] + [self.along(blocks[shift], shift) for shift in range(1, self.own)]
        return total(blocks)

    def chips_sum(self, value):
        by_step = [value] + [self.chip(value, step) for step in range(1, 4)]
        return self.beyond((by_step[0] + by_step[1]) + (by_step[2] + by_step[3]))

    def planes_sum(self, value):
        arrived = [value] + [self.along(value, shift) for shift in range(1, self.own)]
        while len(arrived) > 1:
            half = len(arrived) // 2
            arrived = [a + b for a, b in zip(arrived[:half], arrived[half:])]
        return arrived[0]


def from_behind(block, axis, distance):
    devices = range(lax.axis_size(axis))
    route = [(i - distance, i) for i in devices if i - distance in devices]
    return lax.ppermute(block, axis, route)


def rotation_tables(places):
    half_head = HEAD // 2
    frequency = ROPE_BASE ** (-(jnp.arange(half_head, dtype=F32) * 2.0 / HEAD))
    angles = places.astype(F32)[:, None] * frequency
    cosine, sine = jnp.cos(angles), jnp.sin(angles)
    return jnp.concatenate([cosine] * 4, axis=1), jnp.concatenate([-sine, sine] * 2, axis=1)


def layer_step(
    tokens,
    cotangent,
    segment_ids,
    positions,
    assignment,
    weight_state,
    momentum_state,
    gains,
    gain_momentum,
):
    links = Links()
    weight_lines = weight_state.reshape(-1, LANES)
    moment_lines = momentum_state.reshape(-1, LANES)
    x, turned_up = tokens[0], cotangent[0].T
    places = positions[0]

    first = extract_first(weight_lines)
    near, far = extract_rest(assignment, weight_lines)
    first_line = links.line(first)
    first_line, near = lax.optimization_barrier((first_line, near))
    near_line = links.line(near)
    near_line, far = lax.optimization_barrier((near_line, far))
    far_line = links.line(far)
    w_first, w_first_other = links.spread(links.pick(first_line, assignment[0]))
    near = pick_pieces(assignment, near_line)
    far = pick_pieces(assignment, far_line)
    w_near, w_near_other = links.spread(near)
    w_far, w_far_other = links.spread(far)

    cosine, sine = rotation_tables(places)
    normed, q, k, v, kv, tail, begin = project(x, gains, positions, cosine, sine, w_first, w_first_other)
    kv_prior = from_behind(kv, "cp", 1)
    tops, sums, mixes = attend_own(q, k, v, begin)
    mixed, logs, k_prior, v_prior = attend_prior(places, q, kv_prior, begin, tops, sums, mixes)
    middle, normed_two, turned_two, upstream, w_out, out, back, near_keep, near_send = feed_near(
        x, mixed, tail, turned_up, gains, w_near, w_near_other
    )
    output, grad_middle, grad_mixed, dots, gain_two, grad_tail, far_keep, far_send = feed_far(
        middle, normed_two, turned_two, upstream, turned_up, gains, mixed, w_out, out, back, w_far, w_far_other
    )
    kv_send, query_part = back_prior(places, q, k_prior, v_prior, grad_mixed, logs, dots, positions)
    kv_later = from_behind(kv_send, "cp", -1)
    kv_own, query_grad = back_own(q, k, v, grad_mixed, logs, dots, positions, query_part)
    first_keep, first_send, packed = first_grads(kv_own, kv_later, query_grad, cosine, sine, normed, grad_tail)
    input_grad, output, gain_one = input_grad_of(x, gains, packed, w_first, w_first_other, grad_middle, output)

    def reduced(keep, send):
        parts = links.plane_parts(keep, send)
        blocks = by_plane(links.own, assignment, parts)
        return links.spread(links.line_sum(blocks))

    g_near = reduced(near_keep, near_send)
    g_far = reduced(far_keep, far_send)
    first_sum = total(links.plane_parts(first_keep, first_send))
    g_first = links.spread(links.line_sum([first_sum] * links.own))
    gain_grad = links.chips_sum(jnp.concatenate([gain_one, gain_two], axis=0))
    gain_grad = links.planes_sum(gain_grad)
    gain_grad = gain_grad + links.partner(gain_grad)
    weight_next, moment_state, grad_state = prepare(assignment, weight_lines, moment_lines)
    grad_state, moment_state = ff_lines(assignment, *g_near, *g_far, moment_lines, grad_state, moment_state)
    grad_state, moment_state = attention_lines_update(
        assignment, *g_first, *g_far, moment_lines, grad_state, moment_state
    )
    ortho = orthogonalize(assignment, grad_state, moment_state)
    received = links.partner(ortho)
    weight_next = weight_update(0, assignment, weight_lines, ortho, weight_next)
    weight_next = weight_update(1, assignment, weight_lines, received, weight_next)
    gain_moment = MOMENTUM * gain_momentum + gain_grad
    push_gain = gain_grad + MOMENTUM * gain_moment
    gains_new = gains - GAIN_RATE * push_gain * lax.rsqrt(
        jnp.mean(push_gain * push_gain, axis=-1, keepdims=True) + 1e-06
    )
    return (
        output.T[None],
        input_grad.T[None],
        grad_state.reshape(weight_state.shape),
        weight_next.reshape(weight_state.shape),
        moment_state.reshape(weight_state.shape),
        gain_grad,
        gains_new,
        gain_moment,
    )


def solution(mesh):
    placed = (
        P(("rep", "own"), "cp", None),
        P(("rep", "own"), "cp", None),
        P(("rep", "own"), "cp"),
        P(("rep", "own"), "cp"),
        P(),
        P("own", None),
        P("own", None),
        P(),
        P(),
    )
    return jax.shard_map(
        layer_step,
        mesh=mesh,
        in_specs=placed,
        out_specs=(
            P(("rep", "own"), "cp", None),
            P(("rep", "own"), "cp", None),
            P("own", None),
            P("own", None),
            P("own", None),
            P(),
            P(),
            P(),
        ),
        check_vma=False,
    )
```
